256 devices in a mesh: ckpt: 8 (over y_hi, x), fsdp: 32 (over y_lo, z, core).
Axes of the slice: x: 4, y: 4 (y_hi: 2, y_lo: 2; y = y_hi * 2 + y_lo), z: 8, core: 2. Of those that a mesh axis runs over, the one named last changes fastest.
Arguments:
- tokens: bfloat16 [8, 256, 4096], P('ckpt', 'fsdp'), may hold values from -6 to 6
- gate_weight: bfloat16 [8, 14336, 4096], P('ckpt', 'fsdp'), may hold values from -6 to 6
- up_weight: bfloat16 [8, 14336, 4096], P('ckpt', 'fsdp'), may hold values from -6 to 6
- down_weight: bfloat16 [8, 14336, 4096], P('ckpt', 'fsdp'), may hold values from -0.046875 to 0.046875
- row_code: int32 [8, 2, 4096], P('ckpt'), may hold values from 0 to 2097151
- col_code: int32 [8, 2, 14336], P('ckpt', None, 'fsdp'), may hold values from 0 to 2097151
Outputs:
- merged_gate: bfloat16 [14336, 4096], P('fsdp', 'ckpt')
- merged_up: bfloat16 [14336, 4096], P('fsdp', 'ckpt')
The draws below stay inside these ranges and needn't reach their ends.
All inputs are finite; a program needn't handle non-finite values.
Results may differ from the reference program's by a relative error of at most 0.028.
Values may be sent and summed in bfloat16 or wider, within the bound.
A program may use at most 128 MiB of HBM per device.

```python
import jax
import jax.numpy as jnp
from jax import lax

D = 4096
FF = 14336
TOKENS = 256
CKPT = 8
N_CKPT = 8


def set_ends(entries, stream_key, low, top_value):
    dims = entries.shape
    spot = [jax.random.randint(jax.random.fold_in(stream_key, axis), (), 0, dims[axis]) for axis in range(len(dims))]
    entries = entries.at[tuple(spot)].set(low)
    longest = dims.index(max(dims))
    spot[longest] = (spot[longest] + 1) % dims[longest]
    return entries.at[tuple(spot)].set(top_value)


def levels(key, extent, split, smallest, largest):
    def one(axis_at, parts):
        draws = jax.random.uniform(jax.random.fold_in(jax.random.fold_in(key, 6), axis_at), (parts,), jnp.float32, smallest / len(split), largest / len(split))
        return jnp.repeat(jnp.exp(draws), extent[axis_at] // parts).reshape((-1,) + (1,) * (len(extent) - axis_at - 1))

    level = one(*split[0])
    for cut in split[1:]:
        level = level * one(*cut)
    return level


def centred(key, shape, spread, reach, pieces=(), kind=jnp.bfloat16):
    factor_of = levels(key, shape, pieces, -0.22, 0.18) if pieces else 1.0
    array = jax.random.normal(key, shape, jnp.float32) * spread * factor_of
    return jnp.minimum(jnp.maximum(array, -reach), reach).astype(kind)


def setup_inputs(seed: int = 0) -> dict:
    key_of = jax.random.split(jax.random.key(seed), 7)
    tokens = centred(key_of[0], (CKPT, TOKENS, D), 1.0, 6.0, ((0, 8), (1, 32)))
    gate_weight = centred(key_of[1], (CKPT, FF, D), 1.0, 6.0, ((0, 8), (1, 32)))
    up_weight = centred(key_of[2], (CKPT, FF, D), 1.0, 6.0, ((0, 8), (1, 32)))
    down_weight = centred(key_of[3], (CKPT, FF, D), FF ** -0.5, 0.046875, ((0, 8), (1, 32)))
    row_code = set_ends(jax.random.randint(key_of[4], (CKPT, 2, D), 0, 2097152), jax.random.fold_in(key_of[4], 1), 0, 2097151).astype(jnp.int32)
    col_code = set_ends(jax.random.randint(key_of[5], (CKPT, 2, FF), 0, 2097152), jax.random.fold_in(key_of[5], 1), 0, 2097151).astype(jnp.int32)
    return dict(tokens=tokens, gate_weight=gate_weight, up_weight=up_weight, down_weight=down_weight, row_code=row_code, col_code=col_code)


def odd_bits(value):
    for shift in (16, 8, 4, 2, 1):
        value = jnp.bitwise_xor(value, jnp.right_shift(value, shift))
    return jnp.bitwise_and(value, 1)


def probe(col, row):
    bits = odd_bits(jnp.bitwise_and(col[:, None], row[None, :]))
    return (1 - 2 * bits).astype(jnp.bfloat16)


def cross(left, right):
    return lax.dot_general(left, right, (((1,), (1,)), ((), ())), preferred_element_type=jnp.float32)


def inner(left, right):
    return lax.dot_general(left, right, (((0,), (0,)), ((), ())), preferred_element_type=jnp.float32)


def merge_weight(hessian, signs):
    magnitude = jnp.abs(signs.astype(jnp.float32) * hessian)
    return magnitude / (jnp.mean(magnitude, axis=1, keepdims=True) + 1e-6)


def rounded(value):
    return lax.optimization_barrier(value.astype(jnp.bfloat16)).astype(jnp.float32)


def reference(tokens, gate_weight, up_weight, down_weight, row_code, col_code):
    shape = (FF, D)
    num_gate = jnp.zeros(shape, jnp.float32)
    den_gate = jnp.zeros(shape, jnp.float32)
    num_up = jnp.zeros(shape, jnp.float32)
    den_up = jnp.zeros(shape, jnp.float32)
    factor = D ** -0.5
    for member in range(N_CKPT):
        whole = tokens[member]
        gate = gate_weight[member]
        upper = up_weight[member]
        down = down_weight[member]
        z_gate = probe(col_code[member, 0], row_code[member, 0])
        z_up = probe(col_code[member, 1], row_code[member, 1])
        a_pre = cross(gate, whole) * factor
        b_pre = cross(upper, whole) * factor
        da_pre = cross(z_gate, whole) * factor
        db_pre = cross(z_up, whole) * factor
        sigma = jax.nn.sigmoid(a_pre)
        act = a_pre * sigma
        slope = sigma * (1.0 + a_pre * (1.0 - sigma))
        curve = sigma * (1.0 - sigma) * (2.0 + a_pre * (1.0 - 2.0 * sigma))
        hidden = (act * b_pre).astype(jnp.bfloat16)
        d_hidden = (slope * da_pre * b_pre + act * db_pre).astype(jnp.bfloat16)
        out_y = inner(hidden, down)
        out_dy = inner(d_hidden, down)
        grad_y = out_y.astype(jnp.bfloat16)
        grad_dy = out_dy.astype(jnp.bfloat16)
        grad_h = cross(down, grad_y)
        grad_dh = cross(down, grad_dy)
        dga = (grad_dh * b_pre * slope + grad_h * db_pre * slope + grad_h * b_pre * curve * da_pre).astype(jnp.bfloat16)
        dgb = (grad_dh * act + grad_h * slope * da_pre).astype(jnp.bfloat16)
        hz_gate = jnp.dot(dga, whole, preferred_element_type=jnp.float32)
        hz_up = jnp.dot(dgb, whole, preferred_element_type=jnp.float32)
        w_gate = merge_weight(hz_gate, z_gate)
        w_up = merge_weight(hz_up, z_up)
        num_gate = num_gate + rounded(w_gate * gate.astype(jnp.float32))
        den_gate = den_gate + rounded(w_gate)
        num_up = num_up + rounded(w_up * upper.astype(jnp.float32))
        den_up = den_up + rounded(w_up)
    merged_gate = (num_gate / jnp.maximum(den_gate, 1.0)).astype(jnp.bfloat16)
    merged_up = (num_up / jnp.maximum(den_up, 1.0)).astype(jnp.bfloat16)
    return merged_gate, merged_up
```

```python
import functools

import jax
import jax.numpy as jnp
from jax import lax
from jax.experimental import pallas as pl
from jax.experimental.pallas import tpu as pltpu
from jax.sharding import PartitionSpec as P

NX, NZ = 4, 8
D, FF, TOK = 4096, 448, 256
BLK = 512
ROWS = 112
CHUNKS = FF // ROWS
F32, BF16 = jnp.float32, jnp.bfloat16
DMA = pltpu.SemaphoreType.DMA


def nt(left, right):
    return lax.dot_general(left, right, (((1,), (1,)), ((), ())), preferred_element_type=F32)


def nn(left, right):
    return jnp.dot(left, right, preferred_element_type=F32)


def remote(src, dst, send_sem, recv_sem, device):
    return pltpu.make_async_remote_copy(
        src_ref=src,
        dst_ref=dst,
        send_sem=send_sem,
        recv_sem=recv_sem,
        device_id=device,
        device_id_type=pl.DeviceIdType.MESH,
    )


def activations(a):
    q = lax.logistic(a)
    s = a * q
    s1 = q * (1.0 + a * (1.0 - q))
    s2 = q * (1.0 - q) * (2.0 + a * (1.0 - 2.0 * q))
    return s, s1, s2


def kernel(
    tok, gate, up, down, row, col, out_g, out_u,
    gu_v, w_v, z_v, x_v, xb, wb, pre, hd, h_recv, yp, rs_r, rs_l, y_recv, gy,
    gg, gp, dg, sums, sc, sct, num, den, part, part_recv, row_v, col_v, colt,
    loc, zs, zr, ys, yr, cs, cr, bs, br, ms, rrs, rrr, rls, rlr, es, er,
    ars, arr, als, alr, ds, dr, ss, sr, ps, pr,
):
    ci, fi = lax.axis_index("ckpt"), lax.axis_index("fsdp")
    y_hi, x = ci // NX, ci % NX
    y_lo, z, core = fi // (2 * NZ), (fi % (2 * NZ)) // 2, fi % 2
    row_base = y_lo * (2 * NZ)

    def f_of(yl, zz, cc):
        return (yl * NZ + zz) * 2 + cc

    me = (ci, fi)
    partner = (ci, f_of(y_lo, z, 1 - core))
    y_peer = (ci, f_of(1 - y_lo, z, core))
    hi_peer = ((1 - y_hi) * NX + x, fi)

    def x_peer(i):
        return (y_hi * NX + (x + i) % NX, fi)

    def z_peer(off):
        return (ci, f_of(y_lo, (z + off + NZ) % NZ, core))

    def offset(k):
        return ((k + 1) // 2) * (2 * (k % 2) - 1)

    right, left = z_peer(1), z_peer(-1)

    barrier = pltpu.get_barrier_semaphore()
    everyone = [partner, y_peer, hi_peer]
    everyone += [x_peer(i) for i in (1, 2, 3)] + [z_peer(k) for k in range(1, NZ)]
    for device in everyone:
        pl.semaphore_signal(
            barrier, inc=1, device_id=device, device_id_type=pl.DeviceIdType.MESH
        )
    local = [
        pltpu.make_async_copy(row, row_v, loc.at[0]),
        pltpu.make_async_copy(col, col_v, loc.at[1]),
        pltpu.make_async_copy(tok, x_v.at[pl.ds(fi * 8, 8)], loc.at[2]),
        pltpu.make_async_copy(gate, gu_v.at[0], loc.at[3]),
        pltpu.make_async_copy(up, gu_v.at[1], loc.at[4]),
        pltpu.make_async_copy(down, w_v.at[0], loc.at[5]),
    ]
    own = [pl.ds(pl.multiple_of(BLK * (NX * b + x), BLK), BLK) for b in range(2)]
    for b in range(2):
        mine = xb.at[x * 2 + b, pl.ds(fi * 8, 8)]
        local.append(pltpu.make_async_copy(tok.at[:, own[b]], mine, loc.at[6 + b]))
    for b in range(2):
        local.append(pltpu.make_async_copy(gate.at[:, own[b]], wb.at[x, 0, b], loc.at[8 + b]))
        local.append(pltpu.make_async_copy(up.at[:, own[b]], wb.at[x, 1, b], loc.at[10 + b]))
    for copy in local:
        copy.start()
    pl.semaphore_wait(barrier, len(everyone))

    def tokens_at(which, ff):
        if which == 0:
            return x_v.at[pl.ds(pl.multiple_of(ff * 8, 8), 8)]
        return xb.at[:, pl.ds(pl.multiple_of(ff * 8, 8), 8)]

    def z_copy(which, k, src=None):
        block = tokens_at(which, fi)
        return remote(
            block if src is None else src, block, zs.at[which, k], zr.at[which, k],
            z_peer(offset(k)),
        )

    def z_arrived(which, k):
        block = tokens_at(which, f_of(y_lo, (z - offset(k) + NZ) % NZ, core))
        remote(block, block, zs.at[which, k], zr.at[which, k], z_peer(offset(k))).wait_recv()

    def y_copy(which, k, yl):
        block = tokens_at(which, f_of(yl, (z - offset(k) + NZ) % NZ, core))
        return remote(block, block, ys.at[which, k], yr.at[which, k], y_peer)

    def c_copy(which, k, yl, side, cc):
        block = tokens_at(which, f_of(yl, (z - offset(k) + NZ) % NZ, cc))
        return remote(block, block, cs.at[which, side, k], cr.at[which, side, k], partner)

    def to_z(k, carry):
        z_copy(0, k, tok).start()
        return carry

    local[2].wait()
    y_copy(0, 0, y_lo).start()
    lax.fori_loop(1, NZ, to_z, 0)
    c_copy(0, 0, y_lo, 0, core).start()

    small = []
    for i in (1, 3, 2):
        for b in range(2):
            at = pl.ds(pl.multiple_of(BLK * (NX * b + (x + i) % NX), BLK), BLK)
            small.append(
                remote(
                    tok.at[:, at], xb.at[x * 2 + b, pl.ds(fi * 8, 8)],
                    ms.at[0, i, b], ms.at[1, i, b], x_peer(i),
                )
            )
            small[-1].start()
    down_copy = remote(down, w_v.at[1], ms.at[0, 0, 0], ms.at[1, 0, 0], partner)
    down_copy.start()
    bulk = []
    for k, b in ((0, 0), (1, 0), (0, 1), (1, 1)):
        for i in (1, 3, 2):
            at = pl.ds(pl.multiple_of(BLK * (NX * b + (x + i) % NX), BLK), BLK)
            bulk.append(
                remote(
                    (gate, up)[k].at[:, at], wb.at[x, k, b], bs.at[i, k, b], br.at[i, k, b],
                    x_peer(i),
                )
            )
            bulk[-1].start()

    local[0].wait()
    local[1].wait()
    for k in range(2):
        codes = jnp.concatenate(
            [col_v[k : k + 1, :], jnp.zeros((1, 512 - FF), jnp.int32)], axis=1
        )
        colt[k] = jnp.broadcast_to(codes, (128, 512)).T

    def probe_rows(at, count):
        for k in range(2):
            @pl.loop(0, count)
            def _(t):
                rows = pl.ds(pl.multiple_of(at + t * 16, 16), 16)
                code = colt[k, rows, :]
                for d in range(0, D, 512):
                    wide = jnp.concatenate([code] * 4, axis=1)
                    bits = lax.population_count(
                        jnp.bitwise_and(wide, row_v[k : k + 1, d : d + 512])
                    )
                    sign = 1 - 2 * jnp.bitwise_and(bits, 1)
                    z_v[k, rows, d : d + 512] = sign.astype(F32).astype(BF16)

    def on_z(k, carry):
        z_arrived(0, k)
        y_copy(0, k, y_lo).start()
        c_copy(0, k, y_lo, 0, core).start()
        probe_rows((k - 1) * 64, 4)
        return carry

    lax.fori_loop(1, NZ, on_z, 0)
    local[6].wait()
    local[7].wait()
    for copy in small:
        copy.wait_recv()

    def on_y(which):
        def body(k, carry):
            y_copy(which, k, 1 - y_lo).wait_recv()
            c_copy(which, k, 1 - y_lo, 1, core).start()
            return carry

        return body

    def on_c(which):
        def body(k, carry):
            c_copy(which, k, y_lo, 0, 1 - core).wait_recv()
            c_copy(which, k, 1 - y_lo, 1, 1 - core).wait_recv()
            return carry

        return body

    lax.fori_loop(0, NZ, on_y(0), 0)
    y_copy(1, 0, y_lo).start()
    c_copy(1, 0, y_lo, 0, core).start()

    def to_z_more(k, carry):
        z_copy(1, k).start()
        return carry

    lax.fori_loop(1, NZ, to_z_more, 0)
    local[3].wait()
    local[4].wait()
    lax.fori_loop(0, NZ, on_c(0), 0)

    pre[...] = jnp.zeros_like(pre)

    @pl.loop(0, 4)
    def _(t):
        at = pl.ds(pl.multiple_of(t * 1024, 1024), 1024)
        toks = x_v[:, at]
        pre[0] += nt(gu_v[0, :, at], toks)
        pre[1] += nt(gu_v[1, :, at], toks)
        pre[2] += nt(z_v[0, :, at], toks)
        pre[3] += nt(z_v[1, :, at], toks)

    factor = D ** (-0.5)
    for at, n in ((0, 128), (128, 128), (256, 128), (384, 64)):
        a, b, da, db = (pre[k, at : at + n, :] * factor for k in range(4))
        s, s1, _ = activations(a)
        h = s * b
        dh = s1 * da * b + s * db
        hd[0, :, at : at + n] = h.T.astype(BF16)
        hd[1, :, at : at + n] = dh.T.astype(BF16)
    h_copy = remote(hd.at[1 - core], h_recv, ms.at[0, 0, 1], ms.at[1, 0, 1], partner)
    h_copy.start()
    local[5].wait()
    down_copy.wait_recv()
    h_copy.wait_recv()

    @pl.loop(0, 8)
    def _(t):
        at = pl.ds(pl.multiple_of(t * 512, 512), 512)
        total = nn(hd[core], w_v[0, :, at]) + nn(h_recv[...], w_v[1, :, at])
        yp[:, at] = total.astype(BF16)

    def on_z_more(k, carry):
        z_arrived(1, k)
        y_copy(1, k, y_lo).start()
        c_copy(1, k, y_lo, 0, core).start()
        return carry

    lax.fori_loop(1, NZ, on_z_more, 0)

    def piece(k, half):
        return pl.ds(pl.multiple_of(((z + k + NZ) % NZ) * 32 + 16 * half, 16), 16)

    half_rows = (slice(0, 16), slice(16, 32))

    def send_r(k, half):
        remote(
            yp.at[piece(k, half)], rs_r.at[4 - k, pl.ds(16 * half, 16)],
            rrs.at[4 - k, half], rrr.at[4 - k, half], right,
        ).start()

    def send_l(k, half):
        remote(
            yp.at[piece(-k, half)], rs_l.at[4 - k, pl.ds(16 * half, 16)],
            rls.at[4 - k, half], rlr.at[4 - k, half], left,
        ).start()

    def add_r(k, half):
        slot = rs_r.at[3 - k, pl.ds(16 * half, 16)]
        remote(slot, slot, rrs.at[3 - k, half], rrr.at[3 - k, half], right).wait_recv()
        at = piece(k, half)
        yp[at, :] = (yp[at, :].astype(F32) + rs_r[3 - k, half_rows[half], :].astype(F32)).astype(BF16)

    def add_l(k, half):
        slot = rs_l.at[3 - k, pl.ds(16 * half, 16)]
        remote(slot, slot, rls.at[3 - k, half], rlr.at[3 - k, half], left).wait_recv()
        at = piece(-k, half)
        yp[at, :] = (yp[at, :].astype(F32) + rs_l[3 - k, half_rows[half], :].astype(F32)).astype(BF16)

    send_r(4, 0)
    send_l(4, 1)
    send_r(3, 1)
    send_l(3, 0)
    add_r(3, 0)
    send_r(3, 0)
    add_l(3, 1)
    send_l(3, 1)
    for k in (2, 1):
        for half in (1, 0):
            add_r(k, half)
            send_r(k, half)
            add_l(k, 1 - half)
            send_l(k, 1 - half)
    mine = [piece(0, 0), piece(0, 1)]

    def y_exchange(half):
        return remote(
            yp.at[mine[half]], y_recv.at[pl.ds(16 * half, 16)], es.at[half], er.at[half], y_peer
        )

    add_r(0, 1)
    add_l(0, 0)
    add_l(0, 1)
    y_exchange(1).start()
    add_r(0, 0)
    y_exchange(0).start()

    def gather_copy(k, half, sign):
        at = piece(-sign * (k - 1), half)
        sems = (ars, arr) if sign == 1 else (als, alr)
        return remote(
            gy.at[at], gy.at[at], sems[0].at[k - 1, half], sems[1].at[k - 1, half],
            right if sign == 1 else left,
        )

    def gather_arrived(k, half, sign):
        at = piece(-sign * k, half)
        sems = (ars, arr) if sign == 1 else (als, alr)
        remote(
            gy.at[at], gy.at[at], sems[0].at[k - 1, half], sems[1].at[k - 1, half],
            right if sign == 1 else left,
        ).wait_recv()

    for half in (1, 0):
        y_exchange(half).wait_recv()
        gy[mine[half], :] = (
            yp[mine[half], :].astype(F32) + y_recv[half_rows[half], :].astype(F32)
        ).astype(BF16)
        gather_copy(1, half, 1).start()
        gather_copy(1, half, -1).start()
    for k in (1, 2, 3, 4):
        for half in (1, 0):
            if k < 4 or half == 0:
                gather_arrived(k, half, 1)
            if k < 3 or (k == 3 and half == 0):
                gather_copy(k + 1, half, 1).start()
            if k < 4 or half == 1:
                gather_arrived(k, half, -1)
            if k < 3 or (k == 3 and half == 1):
                gather_copy(k + 1, half, -1).start()
        if k == 1:
            lax.fori_loop(0, NZ, on_y(1), 0)
        if k == 2:
            num[...] = jnp.zeros_like(num)
            den[...] = jnp.zeros_like(den)
            sums[...] = jnp.zeros_like(sums)

    def from_gradient(side, out):
        out[...] = jnp.zeros((FF, TOK), F32)

        @pl.loop(0, 4)
        def _(t):
            at = pl.ds(pl.multiple_of(t * 1024, 1024), 1024)
            out[...] += nt(w_v[side, :, at], gy[:, at])

    from_gradient(1, gp)
    g_copy = remote(gp, gg.at[core], ms.at[0, 0, 2], ms.at[1, 0, 2], partner)
    g_copy.start()
    from_gradient(0, gg.at[core])
    g_back = remote(gp, gg.at[1 - core], ms.at[0, 0, 2], ms.at[1, 0, 2], partner)
    g_back.wait_recv()

    def gradients(at):
        n = ROWS
        a, b, da, db = (pre[k, pl.ds(at, n), :] * factor for k in range(4))
        gh, dgh = gg[0, pl.ds(at, n), :], gg[1, pl.ds(at, n), :]
        s, s1, s2 = activations(a)
        dga = dgh * b * s1 + gh * db * s1 + gh * b * s2 * da
        dgb = dgh * s + gh * s1 * da
        dg[x, 0, pl.ds(at, n), :] = dga.astype(BF16)
        dg[x, 1, pl.ds(at, n), :] = dgb.astype(BF16)

    def dg_copy(r, i):
        at = pl.ds(pl.multiple_of(r * ROWS, ROWS), ROWS)
        return remote(
            dg.at[x, :, at], dg.at[x, :, at], ds.at[r, i], dr.at[r, i], x_peer(i)
        )

    def dg_arrived(r, i):
        at = pl.ds(pl.multiple_of(r * ROWS, ROWS), ROWS)
        got = dg.at[(x - i + NX) % NX, :, at]
        remote(got, got, ds.at[r, i], dr.at[r, i], x_peer(i)).wait_recv()

    @pl.loop(0, CHUNKS)
    def _(r):
        gradients(pl.multiple_of(r * ROWS, ROWS))

    for i in (1, 3, 2):
        dg_copy(0, i).start()

    @pl.loop(0, 8)
    def _(t):
        at = pl.ds(pl.multiple_of(t * 512, 512), 512)
        for k in range(2):
            e = jnp.abs(nn(dg[x, k], x_v[:, at]))
            sums[k, :FF, :] += (e[:, :128] + e[:, 128:256]) + (e[:, 256:384] + e[:, 384:])

    for k in range(2):
        mean = jnp.sum(sums[k].T, axis=0, keepdims=True) * (1.0 / D)
        sc[x, k : k + 1, :] = 1.0 / (mean + 1e-06)

    def sc_copy(i):
        return remote(sc.at[x], sc.at[x], ss.at[i], sr.at[i], x_peer(i))

    def sc_arrived(i):
        got = sc.at[(x - i + NX) % NX]
        remote(got, got, ss.at[i], sr.at[i], x_peer(i)).wait_recv()

    for i in (1, 3, 2):
        sc_copy(i).start()
    for r in range(1, CHUNKS):
        for i in (1, 3, 2):
            dg_copy(r, i).start()

    lax.fori_loop(0, NZ, on_c(1), 0)
    for copy in local[8:]:
        copy.wait()
    for copy in bulk:
        copy.wait_recv()

    for i in (0, 1, 3, 2):
        if i:
            sc_arrived(i)
        peer = (x - i + NX) % NX
        for k in range(2):
            sct[peer, k] = jnp.broadcast_to(sc[peer, k : k + 1, :], (128, 512)).T

    def part_copy(r):
        return remote(part.at[r], part_recv.at[r], ps.at[r], pr.at[r], hi_peer)

    @pl.loop(0, CHUNKS)
    def _(r):
        at = pl.ds(pl.multiple_of(r * ROWS, ROWS), ROWS)

        @pl.loop(0, NX)
        def _(i):
            peer = (x - i + NX) % NX

            @pl.when(i > 0)
            def _():
                dg_arrived(r, i)

            for k in range(2):
                scale = jnp.concatenate([sct[peer, k, at, :]] * 4, axis=1)
                left_side = dg[peer, k, at, :]
                for b in range(2):
                    w = jnp.abs(nn(left_side, xb[peer * 2 + b])) * scale
                    den[b, k, at, :] += w.astype(BF16).astype(F32)
                    term = w * wb[peer, k, b, at, :].astype(F32)
                    num[b, k, at, :] += term.astype(BF16).astype(F32)

        for k in range(2):
            part[r, k, 0] = num[1 - y_hi, k, at, :].astype(BF16)
            part[r, k, 1] = den[1 - y_hi, k, at, :].astype(BF16)
        part_copy(r).start()

    @pl.loop(0, CHUNKS)
    def _(r):
        at = pl.ds(pl.multiple_of(r * ROWS, ROWS), ROWS)
        part_copy(r).wait_recv()
        for k, out in enumerate((out_g, out_u)):
            n = num[y_hi, k, at, :] + part_recv[r, k, 0].astype(F32)
            d = den[y_hi, k, at, :] + part_recv[r, k, 1].astype(F32)
            out[at, :] = (n / jnp.maximum(d, 1.0)).astype(BF16)

    def sent(k, carry):
        for which in range(2):
            z_copy(which, k).wait_send()
        return carry

    def sent_all(k, carry):
        for which in range(2):
            y_copy(which, k, y_lo).wait_send()
            c_copy(which, k, y_lo, 0, core).wait_send()
            c_copy(which, k, 1 - y_lo, 1, core).wait_send()
        return carry

    lax.fori_loop(1, NZ, sent, 0)
    lax.fori_loop(0, NZ, sent_all, 0)
    for copy in small + bulk + [down_copy, h_copy, g_copy]:
        copy.wait_send()
    for k in (4, 3, 2, 1):
        for half in range(2):
            if k < 4 or half == 0:
                remote(
                    yp.at[piece(k, half)], rs_r.at[4 - k, pl.ds(16 * half, 16)],
                    rrs.at[4 - k, half], rrr.at[4 - k, half], right,
                ).wait_send()
                gather_copy(k, half, 1).wait_send()
            if k < 4 or half == 1:
                remote(
                    yp.at[piece(-k, half)], rs_l.at[4 - k, pl.ds(16 * half, 16)],
                    rls.at[4 - k, half], rlr.at[4 - k, half], left,
                ).wait_send()
                gather_copy(k, half, -1).wait_send()
    for half in range(2):
        y_exchange(half).wait_send()
    for i in (1, 3, 2):
        sc_copy(i).wait_send()
        for r in range(CHUNKS):
            dg_copy(r, i).wait_send()
    for r in range(CHUNKS):
        part_copy(r).wait_send()


def on_device(tokens, gate_weight, up_weight, down_weight, row_code, col_code):
    vm = pltpu.VMEM
    scratch = [
        vm((2, FF, D), BF16),
        vm((2, FF, D), BF16),
        vm((2, FF, D), BF16),
        vm((TOK, D), BF16),
        vm((2 * NX, TOK, BLK), BF16),
        vm((NX, 2, 2, FF, BLK), BF16),
        vm((4, FF, TOK), F32),
        vm((2, TOK, FF), BF16),
        vm((TOK, FF), BF16),
        vm((TOK, D), BF16),
        vm((4, 32, D), BF16),
        vm((4, 32, D), BF16),
        vm((32, D), BF16),
        vm((TOK, D), BF16),
        vm((2, FF, TOK), F32),
        vm((FF, TOK), F32),
        vm((NX, 2, FF, TOK), BF16),
        vm((2, 512, 128), F32),
        vm((NX, 8, 512), F32),
        vm((NX, 2, 512, 128), F32),
        vm((2, 2, FF, BLK), F32),
        vm((2, 2, FF, BLK), F32),
        vm((CHUNKS, 2, 2, ROWS, BLK), BF16),
        vm((CHUNKS, 2, 2, ROWS, BLK), BF16),
        vm((2, D), jnp.int32),
        vm((2, FF), jnp.int32),
        vm((2, 512, 128), jnp.int32),
        DMA((12,)),
        DMA((2, NZ)), DMA((2, NZ)),
        DMA((2, NZ)), DMA((2, NZ)),
        DMA((2, 2, NZ)), DMA((2, 2, NZ)),
        DMA((NX, 2, 2)), DMA((NX, 2, 2)),
        DMA((2, NX, 3)),
        DMA((4, 2)), DMA((4, 2)),
        DMA((4, 2)), DMA((4, 2)),
        DMA((2,)), DMA((2,)),
        DMA((4, 2)), DMA((4, 2)),
        DMA((4, 2)), DMA((4, 2)),
        DMA((CHUNKS, NX)), DMA((CHUNKS, NX)),
        DMA((NX,)), DMA((NX,)),
        DMA((CHUNKS,)), DMA((CHUNKS,)),
    ]
    shape = jax.ShapeDtypeStruct((FF, BLK), BF16)
    return pl.pallas_call(
        kernel,
        out_shape=(shape, shape),
        in_specs=[pl.BlockSpec(memory_space=pltpu.HBM)] * 6,
        out_specs=(pl.BlockSpec(memory_space=vm), pl.BlockSpec(memory_space=vm)),
        scratch_shapes=scratch,
        compiler_params=pltpu.CompilerParams(
            collective_id=0, has_side_effects=True, vmem_limit_bytes=67_043_328
        ),
        name="merge",
    )(tokens[0], gate_weight[0], up_weight[0], down_weight[0], row_code[0], col_code[0])


def solution(mesh):
    return jax.shard_map(
        on_device,
        mesh=mesh,
        in_specs=(
            P("ckpt", "fsdp", None),
            P("ckpt", "fsdp", None),
            P("ckpt", "fsdp", None),
            P("ckpt", "fsdp", None),
            P("ckpt", None, None),
            P("ckpt", None, "fsdp"),
        ),
        out_specs=(P("fsdp", "ckpt"), P("fsdp", "ckpt")),
        check_vma=False,
    )
```

```python
import functools

import jax
import jax.numpy as jnp
from jax import lax
from jax.experimental import pallas as pl
from jax.experimental.pallas import tpu as pltpu
from jax.sharding import PartitionSpec as P

NX, NZ = 4, 8
D, FF, TOK = 4096, 448, 256
BLK = 512
EARLY = 160
LATE = FF - EARLY
ROWS = 144
CHUNKS = LATE // ROWS
F32, BF16 = jnp.float32, jnp.bfloat16
DMA = pltpu.SemaphoreType.DMA


def nt(left, right):
    return lax.dot_general(left, right, (((1,), (1,)), ((), ())), preferred_element_type=F32)


def nn(left, right):
    return jnp.dot(left, right, preferred_element_type=F32)


def remote(src, dst, send_sem, recv_sem, device):
    return pltpu.make_async_remote_copy(
        src_ref=src,
        dst_ref=dst,
        send_sem=send_sem,
        recv_sem=recv_sem,
        device_id=device,
        device_id_type=pl.DeviceIdType.MESH,
    )


def activations(a):
    q = lax.logistic(a)
    s = a * q
    s1 = q * (1.0 + a * (1.0 - q))
    s2 = q * (1.0 - q) * (2.0 + a * (1.0 - 2.0 * q))
    return s, s1, s2


def kernel(
    tok, gate, up, down, row, col, out,
    gu_v, w_v, z_v, x_v, xb, we, wl, pre, hd, h_recv, yp, rs_r, rs_l, y_recv, gy,
    gg, gp, dg, dgo, sums, sc, sct, num, den, part, part_recv, res, row_v, col_v, colt,
    loc, zs, zr, ys, yr, cs, cr, bs, br, ms, rrs, rrr, rls, rlr, es, er,
    ars, arr, als, alr, ds, dr, ss, sr, ps, pr,
):
    ci, fi = lax.axis_index("ckpt"), lax.axis_index("fsdp")
    y_hi, x = ci // NX, ci % NX
    y_lo, z, core = fi // (2 * NZ), (fi % (2 * NZ)) // 2, fi % 2
    row_base = y_lo * (2 * NZ)

    def f_of(yl, zz, cc):
        return (yl * NZ + zz) * 2 + cc

    me = (ci, fi)
    partner = (ci, f_of(y_lo, z, 1 - core))
    y_peer = (ci, f_of(1 - y_lo, z, core))
    hi_peer = ((1 - y_hi) * NX + x, fi)

    def x_peer(i):
        return (y_hi * NX + (x + i) % NX, fi)

    def cross_peer(i):
        return ((1 - y_hi) * NX + (x + i) % NX, fi)

    def block_of(b, i):
        return pl.ds(pl.multiple_of(BLK * (NX * b + (x + i) % NX), BLK), BLK)

    early, late = pl.ds(0, EARLY), pl.ds(EARLY, LATE)

    def z_peer(off):
        return (ci, f_of(y_lo, (z + off + NZ) % NZ, core))

    def offset(k):
        return ((k + 1) // 2) * (2 * (k % 2) - 1)

    right, left = z_peer(1), z_peer(-1)

    barrier = pltpu.get_barrier_semaphore()
    everyone = [partner, y_peer, hi_peer] + [cross_peer(i) for i in (1, 2, 3)]
    everyone += [x_peer(i) for i in (1, 2, 3)] + [z_peer(k) for k in (1, -1, 2, -2)]
    for device in everyone:
        pl.semaphore_signal(
            barrier, inc=1, device_id=device, device_id_type=pl.DeviceIdType.MESH
        )
    local = [
        pltpu.make_async_copy(row, row_v, loc.at[0]),
        pltpu.make_async_copy(col, col_v, loc.at[1]),
        pltpu.make_async_copy(tok, x_v.at[pl.ds(fi * 8, 8)], loc.at[2]),
        pltpu.make_async_copy(gate, gu_v.at[0], loc.at[3]),
        pltpu.make_async_copy(up, gu_v.at[1], loc.at[4]),
        pltpu.make_async_copy(down, w_v.at[0], loc.at[5]),
    ]
    for b in range(2):
        spot = xb.at[x * 2 + b, pl.ds(fi * 8, 8)]
        local.append(pltpu.make_async_copy(tok.at[:, block_of(b, 0)], spot, loc.at[6 + b]))
    for k in range(2):
        w_hbm = (gate, up)[k]
        local.append(
            pltpu.make_async_copy(
                w_hbm.at[early, block_of(y_hi, 0)], we.at[x, k], loc.at[8 + k]
            )
        )
        for b in range(2):
            local.append(
                pltpu.make_async_copy(
                    w_hbm.at[late, block_of(b, 0)], wl.at[x, k, b], loc.at[10 + 2 * k + b]
                )
            )
    for copy in local:
        copy.start()
    pl.semaphore_wait(barrier, len(everyone))

    def tokens_at(which, ff):
        if which == 0:
            return x_v.at[pl.ds(pl.multiple_of(ff * 8, 8), 8)]
        return xb.at[:, pl.ds(pl.multiple_of(ff * 8, 8), 8)]

    def z_copy(which, k, src=None):
        block = tokens_at(which, fi)
        return remote(
            block if src is None else src, block, zs.at[which, k], zr.at[which, k],
            z_peer(offset(k)),
        )

    def z_arrived(which, k):
        block = tokens_at(which, f_of(y_lo, (z - offset(k) + NZ) % NZ, core))
        remote(block, block, zs.at[which, k], zr.at[which, k], z_peer(offset(k))).wait_recv()

    def y_copy(which, k, yl):
        block = tokens_at(which, f_of(yl, (z - offset(k) + NZ) % NZ, core))
        return remote(block, block, ys.at[which, k], yr.at[which, k], y_peer)

    def c_copy(which, k, yl, side, cc):
        block = tokens_at(which, f_of(yl, (z - offset(k) + NZ) % NZ, cc))
        return remote(block, block, cs.at[which, side, k], cr.at[which, side, k], partner)

    def z_onward(which, k, to, slot):
        block = tokens_at(which, f_of(y_lo, (z - offset(k) + NZ) % NZ, core))
        return remote(block, block, zs.at[which, slot], zr.at[which, slot], z_peer(offset(to)))


    local[2].wait()
    y_copy(0, 0, y_lo).start()
    for k in (3, 4, 1, 2):
        z_copy(0, k, tok).start()
    c_copy(0, 0, y_lo, 0, core).start()

    small = []
    for i in (1, 3, 2):
        for b in range(2):
            small.append(
                remote(
                    tok.at[:, block_of(b, i)], xb.at[x * 2 + b, pl.ds(fi * 8, 8)],
                    ms.at[0, i, b], ms.at[1, i, b], x_peer(i),
                )
            )
    for i in range(NX):
        small.append(
            remote(
                tok.at[:, block_of(1 - y_hi, i)], xb.at[2 * NX + x, pl.ds(fi * 8, 8)],
                ms.at[0, i, 3], ms.at[1, i, 3], cross_peer(i),
            )
        )
    for copy in small:
        copy.start()
    down_copy = remote(down, w_v.at[1], ms.at[0, 0, 0], ms.at[1, 0, 0], partner)
    down_copy.start()

    def late_weight(i, k, b):
        return remote(
            (gate, up)[k].at[late, block_of(b, i)], wl.at[x, k, b],
            bs.at[i, k, b], br.at[i, k, b], x_peer(i),
        )

    def early_weight(i, k):
        return remote(
            (gate, up)[k].at[early, block_of(y_hi, i)], we.at[x, k],
            bs.at[i, k, 2], br.at[i, k, 2], x_peer(i),
        )

    def cross_weight(i, k):
        return remote(
            (gate, up)[k].at[early, block_of(1 - y_hi, i)], we.at[NX + x, k],
            bs.at[i, k, 3], br.at[i, k, 3], cross_peer(i),
        )

    bulk = [late_weight(i, 0, 0) for i in (1, 3, 2)]
    bulk += [early_weight(i, k) for k in range(2) for i in (1, 3, 2)]
    for copy in bulk:
        copy.start()
    more = [cross_weight(i, k) for k in range(2) for i in (0, 1, 3, 2)]
    more += [late_weight(i, k, b) for k, b in ((0, 1), (1, 0), (1, 1)) for i in (1, 3, 2)]

    local[0].wait()
    local[1].wait()
    for k in range(2):
        codes = jnp.concatenate(
            [col_v[k : k + 1, :], jnp.zeros((1, 512 - FF), jnp.int32)], axis=1
        )
        colt[k] = jnp.broadcast_to(codes, (128, 512)).T

    def probe_rows(at, count):
        for k in range(2):
            @pl.loop(0, count)
            def _(t):
                rows = pl.ds(pl.multiple_of(at + t * 16, 16), 16)
                code = colt[k, rows, :]
                for d in range(0, D, 512):
                    wide = jnp.concatenate([code] * 4, axis=1)
                    bits = lax.population_count(
                        jnp.bitwise_and(wide, row_v[k : k + 1, d : d + 512])
                    )
                    sign = 1 - 2 * jnp.bitwise_and(bits, 1)
                    z_v[k, rows, d : d + 512] = sign.astype(F32).astype(BF16)

    def z_pass(which, k):
        z_arrived(which, k)
        if k == 3:
            z_onward(which, 3, 1, 5).start()

            @pl.when(core == 0)
            def _():
                z_onward(which, 3, 3, 7).start()

        if k == 4:
            z_onward(which, 4, 2, 6).start()

            @pl.when(core == 1)
            def _():
                z_onward(which, 4, 4, 7).start()

    def spread(which, k):
        y_copy(which, k, y_lo).start()
        c_copy(which, k, y_lo, 0, core).start()

    for k in range(1, NZ):
        z_pass(0, k)
        spread(0, k)
        probe_rows((k - 1) * 64, 4)
    local[6].wait()
    local[7].wait()
    for copy in small:
        copy.wait_recv()

    def on_y(which):
        def body(k, carry):
            y_copy(which, k, 1 - y_lo).wait_recv()
            c_copy(which, k, 1 - y_lo, 1, core).start()
            return carry

        return body

    def on_c(which):
        def body(k, carry):
            c_copy(which, k, y_lo, 0, 1 - core).wait_recv()
            c_copy(which, k, 1 - y_lo, 1, 1 - core).wait_recv()
            return carry

        return body

    lax.fori_loop(0, NZ, on_y(0), 0)
    for k in (3, 4, 1, 2):
        z_copy(1, k).start()
    local[3].wait()
    local[4].wait()
    lax.fori_loop(0, NZ, on_c(0), 0)

    pre[...] = jnp.zeros_like(pre)

    @pl.loop(0, 4)
    def _(t):
        at = pl.ds(pl.multiple_of(t * 1024, 1024), 1024)
        toks = x_v[:, at]
        pre[0] += nt(gu_v[0, :, at], toks)
        pre[1] += nt(gu_v[1, :, at], toks)
        pre[2] += nt(z_v[0, :, at], toks)
        pre[3] += nt(z_v[1, :, at], toks)

    for copy in more:
        copy.start()
    factor = D ** (-0.5)
    for at, n in ((0, 128), (128, 128), (256, 128), (384, 64)):
        a, b, da, db = (pre[k, at : at + n, :] * factor for k in range(4))
        s, s1, _ = activations(a)
        h = s * b
        dh = s1 * da * b + s * db
        hd[0, :, at : at + n] = h.T.astype(BF16)
        hd[1, :, at : at + n] = dh.T.astype(BF16)
    h_copy = remote(hd.at[1 - core], h_recv, ms.at[0, 0, 1], ms.at[1, 0, 1], partner)
    h_copy.start()
    for k in (3, 4):
        z_pass(1, k)
    local[5].wait()
    down_copy.wait_recv()
    h_copy.wait_recv()

    @pl.loop(0, 8)
    def _(t):
        at = pl.ds(pl.multiple_of(t * 512, 512), 512)
        total = nn(hd[core], w_v[0, :, at]) + nn(h_recv[...], w_v[1, :, at])
        yp[:, at] = total.astype(BF16)


    def piece(k, half):
        return pl.ds(pl.multiple_of(((z + k + NZ) % NZ) * 32 + 16 * half, 16), 16)

    half_rows = (slice(0, 16), slice(16, 32))

    def send_r(k, half):
        remote(
            yp.at[piece(k, half)], rs_r.at[4 - k, pl.ds(16 * half, 16)],
            rrs.at[4 - k, half], rrr.at[4 - k, half], right,
        ).start()

    def send_l(k, half):
        remote(
            yp.at[piece(-k, half)], rs_l.at[4 - k, pl.ds(16 * half, 16)],
            rls.at[4 - k, half], rlr.at[4 - k, half], left,
        ).start()

    def add_r(k, half):
        slot = rs_r.at[3 - k, pl.ds(16 * half, 16)]
        remote(slot, slot, rrs.at[3 - k, half], rrr.at[3 - k, half], right).wait_recv()
        at = piece(k, half)
        yp[at, :] = (yp[at, :].astype(F32) + rs_r[3 - k, half_rows[half], :].astype(F32)).astype(BF16)

    def add_l(k, half):
        slot = rs_l.at[3 - k, pl.ds(16 * half, 16)]
        remote(slot, slot, rls.at[3 - k, half], rlr.at[3 - k, half], left).wait_recv()
        at = piece(-k, half)
        yp[at, :] = (yp[at, :].astype(F32) + rs_l[3 - k, half_rows[half], :].astype(F32)).astype(BF16)

    send_r(4, 0)
    send_l(4, 1)
    send_r(3, 1)
    send_l(3, 0)
    add_r(3, 0)
    send_r(3, 0)
    add_l(3, 1)
    send_l(3, 1)
    for k in (2, 1):
        for half in (1, 0):
            add_r(k, half)
            send_r(k, half)
            add_l(k, 1 - half)
            send_l(k, 1 - half)
    mine = [piece(0, 0), piece(0, 1)]

    def y_exchange(half):
        return remote(
            yp.at[mine[half]], y_recv.at[pl.ds(16 * half, 16)], es.at[half], er.at[half], y_peer
        )

    add_r(0, 1)
    add_l(0, 0)
    add_l(0, 1)
    y_exchange(1).start()
    add_r(0, 0)
    y_exchange(0).start()

    def gather_copy(k, half, sign):
        at = piece(-sign * (k - 1), half)
        sems = (ars, arr) if sign == 1 else (als, alr)
        return remote(
            gy.at[at], gy.at[at], sems[0].at[k - 1, half], sems[1].at[k - 1, half],
            right if sign == 1 else left,
        )

    def gather_arrived(k, half, sign):
        at = piece(-sign * k, half)
        sems = (ars, arr) if sign == 1 else (als, alr)
        remote(
            gy.at[at], gy.at[at], sems[0].at[k - 1, half], sems[1].at[k - 1, half],
            right if sign == 1 else left,
        ).wait_recv()

    for half in (1, 0):
        y_exchange(half).wait_recv()
        gy[mine[half], :] = (
            yp[mine[half], :].astype(F32) + y_recv[half_rows[half], :].astype(F32)
        ).astype(BF16)
        gather_copy(1, half, 1).start()
        gather_copy(1, half, -1).start()
    def sent(k, carry):
        for which in range(2):
            z_copy(which, k).wait_send()
        return carry

    def spread_sent(which):
        def body(k, carry):
            y_copy(which, k, y_lo).wait_send()
            c_copy(which, k, y_lo, 0, core).wait_send()
            c_copy(which, k, 1 - y_lo, 1, core).wait_send()
            return carry

        return body

    def chain_sent():
        for k in (4, 3, 2, 1):
            for half in range(2):
                if k < 4 or half == 0:
                    remote(
                        yp.at[piece(k, half)], rs_r.at[4 - k, pl.ds(16 * half, 16)],
                        rrs.at[4 - k, half], rrr.at[4 - k, half], right,
                    ).wait_send()
                if k < 4 or half == 1:
                    remote(
                        yp.at[piece(-k, half)], rs_l.at[4 - k, pl.ds(16 * half, 16)],
                        rls.at[4 - k, half], rlr.at[4 - k, half], left,
                    ).wait_send()
        for half in range(2):
            y_exchange(half).wait_send()

    for k in (1, 2, 3, 4):
        for half in (1, 0):
            if k < 4 or half == 0:
                gather_arrived(k, half, 1)
            if k < 3 or (k == 3 and half == 0):
                gather_copy(k + 1, half, 1).start()
            if k < 4 or half == 1:
                gather_arrived(k, half, -1)
            if k < 3 or (k == 3 and half == 1):
                gather_copy(k + 1, half, -1).start()
        if k == 1:
            spread(1, 0)
            for j in (3, 4):
                spread(1, j)
            for j in (1, 2, 5, 6, 7):
                z_pass(1, j)
                spread(1, j)
        if k == 2:
            num[...] = jnp.zeros_like(num)
            den[...] = jnp.zeros_like(den)
            sums[...] = jnp.zeros_like(sums)
            lax.fori_loop(1, NZ, sent, 0)
            for copy in small + [down_copy, h_copy]:
                copy.wait_send()
        if k == 3:
            lax.fori_loop(0, NZ, spread_sent(0), 0)
            chain_sent()

    def from_gradient(side, out):
        out[...] = jnp.zeros((FF, TOK), F32)

        @pl.loop(0, 4)
        def _(t):
            at = pl.ds(pl.multiple_of(t * 1024, 1024), 1024)
            out[...] += nt(w_v[side, :, at], gy[:, at])

    from_gradient(1, gp)
    g_copy = remote(gp, gg.at[core], ms.at[0, 0, 2], ms.at[1, 0, 2], partner)
    g_copy.start()
    from_gradient(0, gg.at[core])
    g_back = remote(gp, gg.at[1 - core], ms.at[0, 0, 2], ms.at[1, 0, 2], partner)
    g_back.wait_recv()

    def gradients(at, n):
        rows = pl.ds(at, n)
        a, b, da, db = (pre[k, rows, :] * factor for k in range(4))
        gh, dgh = gg[0, rows, :], gg[1, rows, :]
        s, s1, s2 = activations(a)
        dga = dgh * b * s1 + gh * db * s1 + gh * b * s2 * da
        dgb = dgh * s + gh * s1 * da
        dg[x, 0, rows, :] = dga.astype(BF16)
        dg[x, 1, rows, :] = dgb.astype(BF16)

    @pl.loop(0, 7)
    def _(t):
        gradients(pl.multiple_of(t * 64, 64), 64)

    def late_rows(r):
        return pl.ds(EARLY + r * ROWS, ROWS)

    def dg_copy(r, i, slot):
        rows = early if r == CHUNKS else late_rows(r)
        spot = dg.at[slot, :, rows]
        return remote(spot, spot, ds.at[r, i], dr.at[r, i], x_peer(i))

    def over_copy():
        return remote(
            dg.at[x, :, early], dgo.at[x], ds.at[CHUNKS, 0], dr.at[CHUNKS, 0], hi_peer
        )

    def onward_copy(i, slot):
        return remote(
            dgo.at[slot], dgo.at[slot], ds.at[CHUNKS + 1, i], dr.at[CHUNKS + 1, i], x_peer(i)
        )

    def from_peer(i):
        return (x - i + NX) % NX

    over_copy().start()
    for i in (1, 3, 2):
        dg_copy(0, i, x).start()

    lax.fori_loop(0, NZ, on_y(1), 0)

    @pl.loop(0, 8)
    def _(t):
        at = pl.ds(pl.multiple_of(t * 512, 512), 512)
        for k in range(2):
            e = jnp.abs(nn(dg[x, k], x_v[:, at]))
            sums[k, :FF, :] += (e[:, :128] + e[:, 128:256]) + (e[:, 256:384] + e[:, 384:])

    for k in range(2):
        mean = jnp.sum(sums[k].T, axis=0, keepdims=True) * (1.0 / D)
        sc[x, k : k + 1, :] = 1.0 / (mean + 1e-06)

    def sc_copy(i, slot):
        return remote(sc.at[slot], sc.at[slot], ss.at[0, i], sr.at[0, i], x_peer(i))

    def sc_over():
        return remote(sc.at[x], sc.at[NX + x], ss.at[0, 0], sr.at[0, 0], hi_peer)

    def sc_onward(i, slot):
        return remote(sc.at[slot], sc.at[slot], ss.at[1, i], sr.at[1, i], x_peer(i))

    for i in (1, 3, 2):
        sc_copy(i, x).start()
    sc_over().start()
    for r in range(1, CHUNKS + 1):
        for i in (1, 3, 2):
            dg_copy(r, i, x).start()

    lax.fori_loop(0, NZ, on_c(1), 0)
    for copy in local[8:]:
        copy.wait()
    for copy in bulk + more:
        copy.wait_recv()

    def columns(slot):
        return [jnp.broadcast_to(sc[slot, k : k + 1, :], (128, 512)).T for k in range(2)]

    def add_terms(left_side, xs, scale, rows, b, weights):
        n = left_side.shape[1]
        hz = nn(left_side.reshape(2 * n, TOK), xs)
        for k in range(2):
            w = jnp.abs(hz[k * n : (k + 1) * n]) * jnp.concatenate([scale(k)] * 4, axis=1)
            den[b, k, rows, :] += w.astype(BF16).astype(F32)
            term = w * weights(k).astype(F32)
            num[b, k, rows, :] += term.astype(BF16).astype(F32)

    def part_copy(r):
        return remote(part.at[r], part_recv.at[r], ps.at[r], pr.at[r], hi_peer)

    for r in range(CHUNKS):
        rows = late_rows(r)

        @pl.loop(0, NX)
        def _(i):
            peer = from_peer(i)

            @pl.when(i > 0)
            def _():
                if r == 0:
                    sc_copy(i, peer).wait_recv()
                dg_copy(r, i, peer).wait_recv()

            if r == 0:
                for k, column in enumerate(columns(peer)):
                    sct[peer, k] = column
            for b in range(2):
                add_terms(
                    dg[peer, :, rows, :], xb[peer * 2 + b], lambda k: sct[peer, k, rows, :],
                    rows, b, lambda k: wl[peer, k, b, r * ROWS : (r + 1) * ROWS, :],
                )

        for k in range(2):
            part[r, k, 0] = num[1 - y_hi, k, rows, :].astype(BF16)
            part[r, k, 1] = den[1 - y_hi, k, rows, :].astype(BF16)
        part_copy(r).start()
        if r == 0:
            over_copy().wait_recv()
            sc_over().wait_recv()
            for i in (1, 3, 2):
                onward_copy(i, x).start()
                sc_onward(i, NX + x).start()

    @pl.loop(0, NX)
    def _(i):
        peer = from_peer(i)

        @pl.when(i > 0)
        def _():
            dg_copy(CHUNKS, i, peer).wait_recv()

        add_terms(
            dg[peer, :, early, :], xb[peer * 2 + y_hi], lambda k: sct[peer, k, early, :],
            early, y_hi, lambda k: we[peer, k],
        )

    @pl.loop(0, NX)
    def _(i):
        peer = from_peer(i)

        @pl.when(i > 0)
        def _():
            onward_copy(i, peer).wait_recv()
            sc_onward(i, NX + peer).wait_recv()

        for k, column in enumerate(columns(NX + peer)):
            sct[peer, k] = column
        add_terms(
            dgo[peer], xb[2 * NX + peer], lambda k: sct[peer, k, early, :],
            early, y_hi, lambda k: we[NX + peer, k],
        )

    def out_copy(r):
        rows = early if r == CHUNKS else late_rows(r)
        return pltpu.make_async_copy(res.at[:, rows], out.at[:, rows], loc.at[r])

    for k in range(2):
        n, d = num[y_hi, k, early, :], den[y_hi, k, early, :]
        res[k, early, :] = (n / jnp.maximum(d, 1.0)).astype(BF16)
    out_copy(CHUNKS).start()

    lax.fori_loop(0, NZ, spread_sent(1), 0)
    for copy in bulk + more + [g_copy, over_copy(), sc_over()]:
        copy.wait_send()
    for k in (4, 3, 2, 1):
        for half in range(2):
            if k < 4 or half == 0:
                gather_copy(k, half, 1).wait_send()
            if k < 4 or half == 1:
                gather_copy(k, half, -1).wait_send()
    for i in (1, 3, 2):
        sc_copy(i, x).wait_send()
        sc_onward(i, NX + x).wait_send()
        onward_copy(i, x).wait_send()
        for r in range(CHUNKS + 1):
            dg_copy(r, i, x).wait_send()

    for r in range(CHUNKS):
        rows = late_rows(r)
        part_copy(r).wait_recv()
        for k in range(2):
            n = num[y_hi, k, rows, :] + part_recv[r, k, 0].astype(F32)
            d = den[y_hi, k, rows, :] + part_recv[r, k, 1].astype(F32)
            res[k, rows, :] = (n / jnp.maximum(d, 1.0)).astype(BF16)
        out_copy(r).start()
    for r in range(CHUNKS):
        part_copy(r).wait_send()
    for r in range(CHUNKS + 1):
        out_copy(r).wait()


def split_out(both, out_g, out_u, buf, sems):
    def read(k):
        return pltpu.make_async_copy(both.at[k], buf.at[k], sems.at[0, k])

    def write(k):
        return pltpu.make_async_copy(buf.at[k], (out_g, out_u)[k], sems.at[1, k])

    for k in range(2):
        read(k).start()
    for k in range(2):
        read(k).wait()
        write(k).start()
    for k in range(2):
        write(k).wait()


def on_device(tokens, gate_weight, up_weight, down_weight, row_code, col_code):
    vm = pltpu.VMEM
    scratch = [
        vm((2, FF, D), BF16),
        vm((2, FF, D), BF16),
        vm((2, FF, D), BF16),
        vm((TOK, D), BF16),
        vm((3 * NX, TOK, BLK), BF16),
        vm((2 * NX, 2, EARLY, BLK), BF16),
        vm((NX, 2, 2, LATE, BLK), BF16),
        vm((4, FF, TOK), F32),
        vm((2, TOK, FF), BF16),
        vm((TOK, FF), BF16),
        vm((TOK, D), BF16),
        vm((4, 32, D), BF16),
        vm((4, 32, D), BF16),
        vm((32, D), BF16),
        vm((TOK, D), BF16),
        vm((2, FF, TOK), F32),
        vm((FF, TOK), F32),
        vm((NX, 2, FF, TOK), BF16),
        vm((NX, 2, EARLY, TOK), BF16),
        vm((2, 512, 128), F32),
        vm((2 * NX, 8, 512), F32),
        vm((NX, 2, 512, 128), F32),
        vm((2, 2, FF, BLK), F32),
        vm((2, 2, FF, BLK), F32),
        vm((CHUNKS, 2, 2, ROWS, BLK), BF16),
        vm((CHUNKS, 2, 2, ROWS, BLK), BF16),
        vm((2, FF, BLK), BF16),
        vm((2, D), jnp.int32),
        vm((2, FF), jnp.int32),
        vm((2, 512, 128), jnp.int32),
        DMA((14,)),
        DMA((2, NZ)), DMA((2, NZ)),
        DMA((2, NZ)), DMA((2, NZ)),
        DMA((2, 2, NZ)), DMA((2, 2, NZ)),
        DMA((NX, 2, 4)), DMA((NX, 2, 4)),
        DMA((2, NX, 4)),
        DMA((4, 2)), DMA((4, 2)),
        DMA((4, 2)), DMA((4, 2)),
        DMA((2,)), DMA((2,)),
        DMA((4, 2)), DMA((4, 2)),
        DMA((4, 2)), DMA((4, 2)),
        DMA((CHUNKS + 2, NX)), DMA((CHUNKS + 2, NX)),
        DMA((2, NX)), DMA((2, NX)),
        DMA((CHUNKS,)), DMA((CHUNKS,)),
    ]
    hbm = pl.BlockSpec(memory_space=pltpu.HBM)
    both = pl.pallas_call(
        kernel,
        out_shape=jax.ShapeDtypeStruct((2, FF, BLK), BF16),
        in_specs=[hbm] * 6,
        out_specs=hbm,
        scratch_shapes=scratch,
        compiler_params=pltpu.CompilerParams(
            collective_id=0, has_side_effects=True, vmem_limit_bytes=67_043_328
        ),
        name="merge",
    )(tokens[0], gate_weight[0], up_weight[0], down_weight[0], row_code[0], col_code[0])
    shape = jax.ShapeDtypeStruct((FF, BLK), BF16)
    return pl.pallas_call(
        split_out,
        out_shape=(shape, shape),
        in_specs=[hbm],
        out_specs=(hbm, hbm),
        scratch_shapes=[vm((2, FF, BLK), BF16), DMA((2, 2))],
        name="split_out",
    )(both)


def solution(mesh):
    return jax.shard_map(
        on_device,
        mesh=mesh,
        in_specs=(
            P("ckpt", "fsdp", None),
            P("ckpt", "fsdp", None),
            P("ckpt", "fsdp", None),
            P("ckpt", "fsdp", None),
            P("ckpt", None, None),
            P("ckpt", None, "fsdp"),
        ),
        out_specs=(P("fsdp", "ckpt"), P("fsdp", "ckpt")),
        check_vma=False,
    )
```

```python
import functools

import jax
import jax.numpy as jnp
from jax import lax
from jax.experimental import pallas as pl
from jax.experimental.pallas import tpu as pltpu
from jax.sharding import PartitionSpec as P

NX, NZ = 4, 8
D, FF, TOK = 4096, 448, 256
BLK = 512
EARLY = 192
LATE = FF - EARLY
ROWS = 64
CHUNKS = LATE // ROWS
F32, BF16 = jnp.float32, jnp.bfloat16
DMA = pltpu.SemaphoreType.DMA


def nt(left, right):
    return lax.dot_general(left, right, (((1,), (1,)), ((), ())), preferred_element_type=F32)


def nn(left, right):
    return jnp.dot(left, right, preferred_element_type=F32)


def remote(src, dst, send_sem, recv_sem, device):
    return pltpu.make_async_remote_copy(
        src_ref=src,
        dst_ref=dst,
        send_sem=send_sem,
        recv_sem=recv_sem,
        device_id=device,
        device_id_type=pl.DeviceIdType.MESH,
    )


def activations(a):
    q = lax.logistic(a)
    s = a * q
    s1 = q * (1.0 + a * (1.0 - q))
    s2 = q * (1.0 - q) * (2.0 + a * (1.0 - 2.0 * q))
    return s, s1, s2


def kernel(
    tok, gate, up, down, row, col, out,
    gu_v, w_v, z_v, x_v, xb, we, wl, pre, hd, h_recv, yp, rs_r, rs_l, y_recv, gy,
    gg, gp, dg, dgo, sums, scl, sc, sct, num, den, part, part_recv, res, row_v, col_v, colt,
    loc, snd, grp, zr, yr, rrr, rlr, er, arr, alr, dr, sr, pr,
):
    ci, fi = lax.axis_index("ckpt"), lax.axis_index("fsdp")
    y_hi, x = ci // NX, ci % NX
    y_lo, z, core = fi // (2 * NZ), (fi % (2 * NZ)) // 2, fi % 2
    row_base = y_lo * (2 * NZ)

    def f_of(yl, zz, cc):
        return (yl * NZ + zz) * 2 + cc

    me = (ci, fi)
    partner = (ci, f_of(y_lo, z, 1 - core))
    y_peer = (ci, f_of(1 - y_lo, z, core))
    hi_peer = ((1 - y_hi) * NX + x, fi)

    def x_peer(i):
        return (y_hi * NX + (x + i) % NX, fi)

    def cross_peer(i):
        return ((1 - y_hi) * NX + (x + i) % NX, fi)

    def block_of(b, i):
        return pl.ds(pl.multiple_of(BLK * (NX * b + (x + i) % NX), BLK), BLK)

    early, late = pl.ds(0, EARLY), pl.ds(EARLY, LATE)

    def z_peer(off):
        return (ci, f_of(y_lo, (z + off + NZ) % NZ, core))

    def offset(k):
        return ((k + 1) // 2) * (2 * (k % 2) - 1)

    right, left = z_peer(1), z_peer(-1)

    def all_sent(ref, sem):
        remote(ref, ref, snd.at[sem], grp.at[0], partner).wait_send()

    def all_here(ref, sem):
        remote(ref, ref, snd.at[0], grp.at[sem], partner).wait_recv()

    barrier = pltpu.get_barrier_semaphore()
    everyone = [partner, y_peer, hi_peer] + [cross_peer(i) for i in (1, 2, 3)]
    everyone += [x_peer(i) for i in (1, 2, 3)] + [z_peer(k) for k in (1, -1, 2, -2)]
    for device in everyone:
        pl.semaphore_signal(
            barrier, inc=1, device_id=device, device_id_type=pl.DeviceIdType.MESH
        )
    local = [
        pltpu.make_async_copy(row, row_v, loc.at[0]),
        pltpu.make_async_copy(col, col_v, loc.at[1]),
        pltpu.make_async_copy(tok, x_v.at[pl.ds(fi * 8, 8)], loc.at[2]),
        pltpu.make_async_copy(gate, gu_v.at[0], loc.at[3]),
        pltpu.make_async_copy(up, gu_v.at[1], loc.at[4]),
        pltpu.make_async_copy(down, w_v.at[0], loc.at[5]),
    ]
    for b in range(2):
        spot = xb.at[x * 2 + b, pl.ds(fi * 8, 8)]
        local.append(pltpu.make_async_copy(tok.at[:, block_of(b, 0)], spot, loc.at[6 + b]))
    for k in range(2):
        w_hbm = (gate, up)[k]
        local.append(
            pltpu.make_async_copy(
                w_hbm.at[early, block_of(y_hi, 0)], we.at[x, k], loc.at[8 + k]
            )
        )
        for b in range(2):
            local.append(
                pltpu.make_async_copy(
                    w_hbm.at[late, block_of(b, 0)], wl.at[x, k, b], loc.at[10 + 2 * k + b]
                )
            )
    for copy in local:
        copy.start()
    pl.semaphore_wait(barrier, len(everyone))

    def tokens_at(which, ff):
        if which == 0:
            return x_v.at[pl.ds(pl.multiple_of(ff * 8, 8), 8)]
        return xb.at[:, pl.ds(pl.multiple_of(ff * 8, 8), 8)]

    def z_copy(which, k, src=None):
        block = tokens_at(which, fi)
        return remote(
            block if src is None else src, block, snd.at[which], zr.at[which, k],
            z_peer(offset(k)),
        )

    def z_arrived(which, k):
        block = tokens_at(which, f_of(y_lo, (z - offset(k) + NZ) % NZ, core))
        remote(block, block, snd.at[which], zr.at[which, k], z_peer(offset(k))).wait_recv()

    def y_copy(which, k, yl):
        block = tokens_at(which, f_of(yl, (z - offset(k) + NZ) % NZ, core))
        return remote(block, block, snd.at[which], yr.at[k] if which == 0 else grp.at[8], y_peer)

    def c_copy(which, k, yl):
        block = tokens_at(which, f_of(yl, (z - offset(k) + NZ) % NZ, core))
        return remote(block, block, snd.at[which], grp.at[which], partner)

    def z_onward(which, k, to, slot):
        block = tokens_at(which, f_of(y_lo, (z - offset(k) + NZ) % NZ, core))
        return remote(block, block, snd.at[which], zr.at[which, slot], z_peer(offset(to)))


    local[2].wait()
    y_copy(0, 0, y_lo).start()
    for k in (1, 2, 3, 4):
        z_copy(0, k, tok).start()
    c_copy(0, 0, y_lo).start()

    small = []
    for i in (1, 3, 2):
        for b in range(2):
            small.append(
                remote(
                    tok.at[:, block_of(b, i)], xb.at[x * 2 + b, pl.ds(fi * 8, 8)],
                    snd.at[2], grp.at[2], x_peer(i),
                )
            )
    for i in range(NX):
        small.append(
            remote(
                tok.at[:, block_of(1 - y_hi, i)], xb.at[2 * NX + x, pl.ds(fi * 8, 8)],
                snd.at[2], grp.at[2], cross_peer(i),
            )
        )
    for copy in small:
        copy.start()
    down_copy = remote(down, w_v.at[1], snd.at[3], grp.at[3], partner)
    down_copy.start()

    def late_weight(i, k, b):
        return remote(
            (gate, up)[k].at[late, block_of(b, i)], wl.at[x, k, b],
            snd.at[8], grp.at[6], x_peer(i),
        )

    def early_weight(i, k):
        return remote(
            (gate, up)[k].at[early, block_of(y_hi, i)], we.at[x, k],
            snd.at[9], grp.at[7], x_peer(i),
        )

    def cross_weight(i, k):
        return remote(
            (gate, up)[k].at[early, block_of(1 - y_hi, i)], we.at[NX + x, k],
            snd.at[9], grp.at[7], cross_peer(i),
        )

    for i in (1, 3, 2):
        late_weight(i, 0, 0).start()
    for i in (1, 3):
        early_weight(i, 0).start()

    local[0].wait()
    local[1].wait()
    for k in range(2):
        codes = jnp.concatenate(
            [col_v[k : k + 1, :], jnp.zeros((1, 512 - FF), jnp.int32)], axis=1
        )
        colt[k] = jnp.broadcast_to(codes, (128, 512)).T

    def probe_rows(at, count):
        for k in range(2):
            @pl.loop(0, count)
            def _(t):
                rows = pl.ds(pl.multiple_of(at + t * 16, 16), 16)
                code = colt[k, rows, :]
                for d in range(0, D, 512):
                    wide = jnp.concatenate([code] * 4, axis=1)
                    bits = lax.population_count(
                        jnp.bitwise_and(wide, row_v[k : k + 1, d : d + 512])
                    )
                    sign = 1 - 2 * jnp.bitwise_and(bits, 1)
                    z_v[k, rows, d : d + 512] = sign.astype(F32).astype(BF16)

    def z_pass(which, k):
        z_arrived(which, k)
        if k == 3:
            z_onward(which, 3, 1, 5).start()

            @pl.when(core == 0)
            def _():
                z_onward(which, 3, 3, 7).start()

        if k == 4:
            z_onward(which, 4, 2, 6).start()

            @pl.when(core == 1)
            def _():
                z_onward(which, 4, 4, 7).start()

    def spread(which, k):
        y_copy(which, k, y_lo).start()
        c_copy(which, k, y_lo).start()

    probe_rows(0, 14)
    for k in (1, 2, 3, 4):
        z_pass(0, k)
        spread(0, k)
    probe_rows(224, 14)
    for k in (5, 6, 7):
        z_pass(0, k)
        spread(0, k)
    local[6].wait()
    local[7].wait()
    all_here(xb.at[0, pl.ds(0, 80)], 2)

    def on_y(k, carry):
        y_copy(0, k, 1 - y_lo).wait_recv()
        c_copy(0, k, 1 - y_lo).start()
        return carry

    lax.fori_loop(0, NZ, on_y, 0)
    for k in (3, 4, 1, 2):
        z_copy(1, k).start()
    local[3].wait()
    local[4].wait()
    all_here(x_v.at[pl.ds(0, 128)], 0)

    for i in (1, 3):
        cross_weight(i, 0).start()
    for i in (1, 3):
        late_weight(i, 0, 1).start()
    cross_weight(2, 0).start()
    for i in (1, 3, 2):
        cross_weight(i, 1).start()
    late_weight(2, 0, 1).start()
    for i in (1, 3, 2):
        late_weight(i, 1, 0).start()
    for i in (1, 3, 2):
        late_weight(i, 1, 1).start()
    for k in range(2):
        early_weight(2, k).start()

    pre[...] = jnp.zeros_like(pre)

    @pl.loop(0, 4)
    def _(t):
        at = pl.ds(pl.multiple_of(t * 1024, 1024), 1024)
        toks = x_v[:, at]
        pre[0] += nt(gu_v[0, :, at], toks)
        pre[1] += nt(gu_v[1, :, at], toks)
        pre[2] += nt(z_v[0, :, at], toks)
        pre[3] += nt(z_v[1, :, at], toks)

    factor = D ** (-0.5)
    for at, n in ((0, 128), (128, 128), (256, 128), (384, 64)):
        a, b, da, db = (pre[k, at : at + n, :] * factor for k in range(4))
        s, s1, _ = activations(a)
        h = s * b
        dh = s1 * da * b + s * db
        hd[0, :, at : at + n] = h.T.astype(BF16)
        hd[1, :, at : at + n] = dh.T.astype(BF16)
    h_copy = remote(hd.at[1 - core], h_recv, snd.at[4], grp.at[4], partner)
    h_copy.start()
    for k in (3, 4):
        z_pass(1, k)
    local[5].wait()
    down_copy.wait_recv()
    h_copy.wait_recv()

    @pl.loop(0, 8)
    def _(t):
        at = pl.ds(pl.multiple_of(t * 512, 512), 512)
        total = nn(hd[core], w_v[0, :, at]) + nn(h_recv[...], w_v[1, :, at])
        yp[:, at] = total.astype(BF16)


    def piece(k, half):
        return pl.ds(pl.multiple_of(((z + k + NZ) % NZ) * 32 + 16 * half, 16), 16)

    half_rows = (slice(0, 16), slice(16, 32))

    def send_r(k, half):
        remote(
            yp.at[piece(k, half)], rs_r.at[4 - k, pl.ds(16 * half, 16)],
            snd.at[6], rrr.at[4 - k, half], right,
        ).start()

    def send_l(k, half):
        remote(
            yp.at[piece(-k, half)], rs_l.at[4 - k, pl.ds(16 * half, 16)],
            snd.at[6], rlr.at[4 - k, half], left,
        ).start()

    def add_r(k, half):
        slot = rs_r.at[3 - k, pl.ds(16 * half, 16)]
        remote(slot, slot, snd.at[6], rrr.at[3 - k, half], right).wait_recv()
        at = piece(k, half)
        yp[at, :] = (yp[at, :].astype(F32) + rs_r[3 - k, half_rows[half], :].astype(F32)).astype(BF16)

    def add_l(k, half):
        slot = rs_l.at[3 - k, pl.ds(16 * half, 16)]
        remote(slot, slot, snd.at[6], rlr.at[3 - k, half], left).wait_recv()
        at = piece(-k, half)
        yp[at, :] = (yp[at, :].astype(F32) + rs_l[3 - k, half_rows[half], :].astype(F32)).astype(BF16)

    send_r(4, 0)
    send_l(4, 1)
    send_r(3, 1)
    send_l(3, 0)
    add_r(3, 0)
    send_r(3, 0)
    add_l(3, 1)
    send_l(3, 1)
    for k in (2, 1):
        for half in (1, 0):
            add_r(k, half)
            send_r(k, half)
            add_l(k, 1 - half)
            send_l(k, 1 - half)
    mine = [piece(0, 0), piece(0, 1)]

    def y_exchange(half):
        return remote(
            yp.at[mine[half]], y_recv.at[pl.ds(16 * half, 16)], snd.at[6], er.at[half], y_peer
        )

    add_r(0, 1)
    add_l(0, 0)
    add_l(0, 1)
    y_exchange(1).start()
    add_r(0, 0)
    y_exchange(0).start()

    def gather_copy(k, half, sign):
        at = piece(-sign * (k - 1), half)
        sem = arr if sign == 1 else alr
        return remote(
            gy.at[at], gy.at[at], snd.at[7], sem.at[k - 1, half],
            right if sign == 1 else left,
        )

    def gather_arrived(k, half, sign):
        at = piece(-sign * k, half)
        sem = arr if sign == 1 else alr
        remote(
            gy.at[at], gy.at[at], snd.at[7], sem.at[k - 1, half],
            right if sign == 1 else left,
        ).wait_recv()

    for half in (1, 0):
        y_exchange(half).wait_recv()
        gy[mine[half], :] = (
            yp[mine[half], :].astype(F32) + y_recv[half_rows[half], :].astype(F32)
        ).astype(BF16)
        gather_copy(1, half, 1).start()
        gather_copy(1, half, -1).start()
    for k in (1, 2, 3, 4):
        for half in (1, 0):
            if k < 4 or half == 0:
                gather_arrived(k, half, 1)
            if k < 3 or (k == 3 and half == 0):
                gather_copy(k + 1, half, 1).start()
            if k < 4 or half == 1:
                gather_arrived(k, half, -1)
            if k < 3 or (k == 3 and half == 1):
                gather_copy(k + 1, half, -1).start()
        if k == 1:
            spread(1, 0)
            for j in (3, 4):
                spread(1, j)
            for j in (1, 2, 5, 6, 7):
                z_pass(1, j)
                spread(1, j)
            for j in range(2):
                cross_weight(0, j).start()
        if k == 2:
            num[...] = jnp.zeros_like(num)
            den[...] = jnp.zeros_like(den)
            sums[...] = jnp.zeros_like(sums)
            all_sent(x_v.at[pl.ds(0, 248)], 0)
            all_sent(xb.at[0, pl.ds(0, 80)], 2)
            all_sent(yp, 6)
            down_copy.wait_send()
            h_copy.wait_send()

    def from_gradient(side, out, rows):
        out[rows, :] = jnp.zeros((rows.size, TOK), F32)

        @pl.loop(0, 4)
        def _(t):
            at = pl.ds(pl.multiple_of(t * 1024, 1024), 1024)
            out[rows, :] += nt(w_v[side, rows, at], gy[:, at])

    def g_copy(group):
        rows = (late, early)[group]
        return remote(
            gp.at[rows], gg.at[core, rows], snd.at[5], (grp.at[5], grp.at[9])[group], partner
        )

    def gradients(at, n):
        rows = pl.ds(at, n)
        a, b, da, db = (pre[k, rows, :] * factor for k in range(4))
        gh, dgh = gg[0, rows, :], gg[1, rows, :]
        s, s1, s2 = activations(a)
        dga = dgh * b * s1 + gh * db * s1 + gh * b * s2 * da
        dgb = dgh * s + gh * s1 * da
        dg[x, 0, rows, :] = dga.astype(BF16)
        dg[x, 1, rows, :] = dgb.astype(BF16)

    def late_rows(r):
        return pl.ds(EARLY + r * ROWS, ROWS)

    def dg_copy(r, i, slot):
        rows = early if r == CHUNKS else late_rows(r)
        spot = dg.at[slot, :, rows]
        return remote(spot, spot, snd.at[10], dr.at[r, i], x_peer(i))

    def over_copy():
        return remote(dg.at[x, :, early], dgo.at[x], snd.at[10], dr.at[CHUNKS, 0], hi_peer)

    def onward_copy(i, slot):
        return remote(dgo.at[slot], dgo.at[slot], snd.at[10], dr.at[CHUNKS + 1, i], x_peer(i))

    def from_peer(i):
        return (x - i + NX) % NX

    def pass_on(cross, i):
        k, slot = (0, 1)[i == 3], from_peer(i)
        spot = dgo.at[slot, k] if cross else dg.at[slot, k, early]
        remote(spot, spot, snd.at[10], dr.at[CHUNKS + cross, 2], x_peer(i)).start()

    def means(group):
        rows = (late, early)[group]

        @pl.loop(0, 8)
        def _(t):
            at = pl.ds(pl.multiple_of(t * 512, 512), 512)
            for k in range(2):
                e = jnp.abs(nn(dg[x, k, rows, :], x_v[:, at]))
                sums[k, rows, :] += (e[:, :128] + e[:, 128:256]) + (e[:, 256:384] + e[:, 384:])

        for k in range(2):
            mean = jnp.sum(sums[k].T, axis=0, keepdims=True) * (1.0 / D)
            (scl, sc)[group][x, k : k + 1, :] = 1.0 / (mean + 1e-06)

    def scl_copy(i, slot):
        return remote(scl.at[slot], scl.at[slot], snd.at[13], sr.at[2, i], x_peer(i))

    def sc_copy(i, slot):
        return remote(sc.at[slot], sc.at[slot], snd.at[11], sr.at[0, i], x_peer(i))

    def sc_over():
        return remote(sc.at[x], sc.at[NX + x], snd.at[11], sr.at[0, 0], hi_peer)

    def sc_onward(i, slot):
        return remote(sc.at[slot], sc.at[slot], snd.at[11], sr.at[1, i], x_peer(i))

    from_gradient(1, gp, late)
    g_copy(0).start()
    from_gradient(0, gg.at[core], late)
    from_gradient(1, gp, early)
    g_copy(1).start()

    def g_arrived(group):
        rows = (late, early)[group]
        remote(
            gp.at[rows], gg.at[1 - core, rows], snd.at[5], (grp.at[5], grp.at[9])[group], partner
        ).wait_recv()

    g_arrived(0)

    @pl.loop(0, LATE // 64)
    def _(t):
        gradients(pl.multiple_of(EARLY + t * 64, 64), 64)

    for i in (1, 3, 2):
        dg_copy(0, i, x).start()
    all_here(xb.at[:, pl.ds(0, 64)], 8)

    @pl.loop(0, NZ)
    def _(k):
        c_copy(1, k, 1 - y_lo).start()

    means(0)
    for i in (1, 3, 2):
        scl_copy(i, x).start()
    for r in range(1, CHUNKS):
        for i in (1, 3, 2):
            dg_copy(r, i, x).start()
    for i in (1, 3):
        early_weight(i, 1).start()
    from_gradient(0, gg.at[core], early)
    g_arrived(1)

    @pl.loop(0, EARLY // 64)
    def _(t):
        gradients(pl.multiple_of(t * 64, 64), 64)

    over_copy().start()
    for i in (1, 3):
        dg_copy(CHUNKS, i, x).start()
    all_here(xb.at[:, pl.ds(0, 128)], 1)
    for copy in local[8:]:
        copy.wait()
    all_here(gu_v.at[0, pl.ds(0, 12 * LATE * BLK // D)], 6)

    def columns(ref, slot):
        return [jnp.broadcast_to(ref[slot, k : k + 1, :], (128, 512)).T for k in range(2)]

    def add_terms(left_side, xs, scale, rows, b, weights):
        n = left_side.shape[1]
        hz = nn(left_side.reshape(2 * n, TOK), xs)
        for k in range(2):
            w = jnp.abs(hz[k * n : (k + 1) * n]) * jnp.concatenate([scale(k)] * 4, axis=1)
            den[b, k, rows, :] += w.astype(BF16).astype(F32)
            term = w * weights(k).astype(F32)
            num[b, k, rows, :] += term.astype(BF16).astype(F32)

    def part_copy(r):
        return remote(part.at[r], part_recv.at[r], snd.at[12], pr.at[r], hi_peer)

    for r in range(CHUNKS):
        rows = late_rows(r)

        @pl.loop(0, NX)
        def _(j):
            i = j ^ (j >> 1)
            peer = from_peer(i)

            @pl.when(i > 0)
            def _():
                if r == 0:
                    scl_copy(i, peer).wait_recv()
                dg_copy(r, i, peer).wait_recv()

            if r == 0:
                for k, column in enumerate(columns(scl, peer)):
                    sct[peer, k] = column
            for b in range(2):
                add_terms(
                    dg[peer, :, rows, :], xb[peer * 2 + b], lambda k: sct[peer, k, rows, :],
                    rows, b, lambda k: wl[peer, k, b, r * ROWS : (r + 1) * ROWS, :],
                )

        for k in range(2):
            part[r, k, 0] = num[1 - y_hi, k, rows, :].astype(BF16)
            part[r, k, 1] = den[1 - y_hi, k, rows, :].astype(BF16)
        part_copy(r).start()
        if r == 0:
            means(1)
            sc_over().start()
            for i in (1, 3, 2):
                sc_copy(i, x).start()
        if r == 2:
            over_copy().wait_recv()
            sc_over().wait_recv()
            for i in (1, 3):
                onward_copy(i, x).start()
            for i in (1, 3, 2):
                sc_onward(i, NX + x).start()

    all_here(gu_v.at[1, pl.ds(0, 14 * EARLY * BLK // D)], 7)

    def early_terms(cross, i):
        peer = from_peer(i)
        slot = NX * cross + peer
        if i:
            (sc_onward if cross else sc_copy)(i, slot).wait_recv()
        column = columns(sc, slot)
        add_terms(
            dgo[peer] if cross else dg[peer, :, early, :],
            xb[2 * NX + peer] if cross else xb[peer * 2 + y_hi],
            lambda k: column[k][:EARLY], early, y_hi, lambda k: we[slot, k],
        )

    early_terms(0, 0)
    for i in (1, 3):
        dg_copy(CHUNKS, i, from_peer(i)).wait_recv()
        pass_on(0, i)
    early_terms(1, 0)
    early_terms(0, 1)
    early_terms(0, 3)
    for i in (1, 3):
        onward_copy(i, from_peer(i)).wait_recv()
        pass_on(1, i)
    early_terms(1, 1)
    early_terms(1, 3)
    dg_copy(CHUNKS, 2, from_peer(2)).wait_recv()
    early_terms(0, 2)
    onward_copy(2, from_peer(2)).wait_recv()
    early_terms(1, 2)

    def out_copy(r):
        rows = early if r == CHUNKS else late_rows(r)
        return pltpu.make_async_copy(res.at[:, rows], out.at[:, rows], loc.at[r])

    for k in range(2):
        n, d = num[y_hi, k, early, :], den[y_hi, k, early, :]
        res[k, early, :] = (n / jnp.maximum(d, 1.0)).astype(BF16)
    out_copy(CHUNKS).start()

    all_sent(xb.at[:, pl.ds(0, 248)], 1)
    all_sent(gu_v.at[0, pl.ds(0, 12 * LATE * BLK // D)], 8)
    all_sent(gu_v.at[1, pl.ds(0, 14 * EARLY * BLK // D)], 9)
    all_sent(gy.at[pl.ds(0, 224)], 7)
    all_sent(gu_v.at[0, pl.ds(0, (3 * LATE + 7 * EARLY) * 2 * TOK // D)], 10)
    all_sent(sc.at[pl.ds(0, 7)], 11)
    all_sent(scl.at[pl.ds(0, 3)], 13)
    all_sent(gp, 5)

    for r in range(CHUNKS):
        rows = late_rows(r)
        part_copy(r).wait_recv()
        for k in range(2):
            n = num[y_hi, k, rows, :] + part_recv[r, k, 0].astype(F32)
            d = den[y_hi, k, rows, :] + part_recv[r, k, 1].astype(F32)
            res[k, rows, :] = (n / jnp.maximum(d, 1.0)).astype(BF16)
        out_copy(r).start()
    all_sent(part, 12)
    for r in range(CHUNKS + 1):
        out_copy(r).wait()


def split_out(both, out_g, out_u, buf, sems):
    def read(k):
        return pltpu.make_async_copy(both.at[k], buf.at[k], sems.at[0, k])

    def write(k):
        return pltpu.make_async_copy(buf.at[k], (out_g, out_u)[k], sems.at[1, k])

    for k in range(2):
        read(k).start()
    for k in range(2):
        read(k).wait()
        write(k).start()
    for k in range(2):
        write(k).wait()


def on_device(tokens, gate_weight, up_weight, down_weight, row_code, col_code):
    vm = pltpu.VMEM
    scratch = [
        vm((2, FF, D), BF16),
        vm((2, FF, D), BF16),
        vm((2, FF, D), BF16),
        vm((TOK, D), BF16),
        vm((3 * NX, TOK, BLK), BF16),
        vm((2 * NX, 2, EARLY, BLK), BF16),
        vm((NX, 2, 2, LATE, BLK), BF16),
        vm((4, FF, TOK), F32),
        vm((2, TOK, FF), BF16),
        vm((TOK, FF), BF16),
        vm((TOK, D), BF16),
        vm((4, 32, D), BF16),
        vm((4, 32, D), BF16),
        vm((32, D), BF16),
        vm((TOK, D), BF16),
        vm((2, FF, TOK), F32),
        vm((FF, TOK), F32),
        vm((NX, 2, FF, TOK), BF16),
        vm((NX, 2, EARLY, TOK), BF16),
        vm((2, 512, 128), F32),
        vm((NX, 8, 512), F32),
        vm((2 * NX, 8, 512), F32),
        vm((NX, 2, 512, 128), F32),
        vm((2, 2, FF, BLK), F32),
        vm((2, 2, FF, BLK), F32),
        vm((CHUNKS, 2, 2, ROWS, BLK), BF16),
        vm((CHUNKS, 2, 2, ROWS, BLK), BF16),
        vm((2, FF, BLK), BF16),
        vm((2, D), jnp.int32),
        vm((2, FF), jnp.int32),
        vm((2, 512, 128), jnp.int32),
        DMA((14,)), DMA((14,)), DMA((10,)),
        DMA((2, NZ)), DMA((NZ,)),
        DMA((4, 2)), DMA((4, 2)), DMA((2,)),
        DMA((4, 2)), DMA((4, 2)),
        DMA((CHUNKS + 2, NX)), DMA((3, NX)), DMA((CHUNKS,)),
    ]
    hbm = pl.BlockSpec(memory_space=pltpu.HBM)
    both = pl.pallas_call(
        kernel,
        out_shape=jax.ShapeDtypeStruct((2, FF, BLK), BF16),
        in_specs=[hbm] * 6,
        out_specs=hbm,
        scratch_shapes=scratch,
        compiler_params=pltpu.CompilerParams(
            collective_id=0, has_side_effects=True, vmem_limit_bytes=67_043_328
        ),
        name="merge",
    )(tokens[0], gate_weight[0], up_weight[0], down_weight[0], row_code[0], col_code[0])
    shape = jax.ShapeDtypeStruct((FF, BLK), BF16)
    return pl.pallas_call(
        split_out,
        out_shape=(shape, shape),
        in_specs=[hbm],
        out_specs=(hbm, hbm),
        scratch_shapes=[vm((2, FF, BLK), BF16), DMA((2, 2))],
        name="split_out",
    )(both)


def solution(mesh):
    return jax.shard_map(
        on_device,
        mesh=mesh,
        in_specs=(
            P("ckpt", "fsdp", None),
            P("ckpt", "fsdp", None),
            P("ckpt", "fsdp", None),
            P("ckpt", "fsdp", None),
            P("ckpt", None, None),
            P("ckpt", None, "fsdp"),
        ),
        out_specs=(P("fsdp", "ckpt"), P("fsdp", "ckpt")),
        check_vma=False,
    )
```

```python
import functools

import jax
import jax.numpy as jnp
from jax import lax
from jax.experimental import pallas as pl
from jax.experimental.pallas import tpu as pltpu
from jax.sharding import PartitionSpec as P

NX, NZ = 4, 8
D, FF, TOK = 4096, 448, 256
BLK = 512
EARLY = 192
LATE = FF - EARLY
ROWS = 64
CHUNKS = LATE // ROWS
F32, BF16 = jnp.float32, jnp.bfloat16
DMA = pltpu.SemaphoreType.DMA


def nt(left, right):
    return lax.dot_general(left, right, (((1,), (1,)), ((), ())), preferred_element_type=F32)


def nn(left, right):
    return jnp.dot(left, right, preferred_element_type=F32)


def remote(src, dst, send_sem, recv_sem, device):
    return pltpu.make_async_remote_copy(
        src_ref=src,
        dst_ref=dst,
        send_sem=send_sem,
        recv_sem=recv_sem,
        device_id=device,
        device_id_type=pl.DeviceIdType.MESH,
    )


def activations(a):
    q = lax.logistic(a)
    s = a * q
    s1 = q * (1.0 + a * (1.0 - q))
    s2 = q * (1.0 - q) * (2.0 + a * (1.0 - 2.0 * q))
    return s, s1, s2


def kernel(
    tok, gate, up, down, row, col, out,
    gu_v, w_v, z_v, x_v, xb, we, wl, pre, hd, h_recv, yp, rs_r, rs_l, y_recv, gy,
    gg, gp, dg, dgo, sums, scl, sc, sct, num, den, part, part_recv, row_v, col_v, colt,
    loc, snd, grp, zr, yr, rrr, rlr, er, arr, alr, dr, sr, pr,
):
    ci, fi = lax.axis_index("ckpt"), lax.axis_index("fsdp")
    y_hi, x = ci // NX, ci % NX
    y_lo, z, core = fi // (2 * NZ), (fi % (2 * NZ)) // 2, fi % 2
    row_base = y_lo * (2 * NZ)

    def f_of(yl, zz, cc):
        return (yl * NZ + zz) * 2 + cc

    me = (ci, fi)
    partner = (ci, f_of(y_lo, z, 1 - core))
    y_peer = (ci, f_of(1 - y_lo, z, core))
    hi_peer = ((1 - y_hi) * NX + x, fi)

    def x_peer(i):
        return (y_hi * NX + (x + i) % NX, fi)

    def cross_peer(i):
        return ((1 - y_hi) * NX + (x + i) % NX, fi)

    def block_of(b, i):
        return pl.ds(pl.multiple_of(BLK * (NX * b + (x + i) % NX), BLK), BLK)

    early, late = pl.ds(0, EARLY), pl.ds(EARLY, LATE)

    def z_peer(off):
        return (ci, f_of(y_lo, (z + off + NZ) % NZ, core))

    def offset(k):
        return ((k + 1) // 2) * (2 * (k % 2) - 1)

    right, left = z_peer(1), z_peer(-1)

    def all_sent(ref, sem):
        remote(ref, ref, snd.at[sem], grp.at[0], partner).wait_send()

    def all_here(ref, sem):
        remote(ref, ref, snd.at[0], grp.at[sem], partner).wait_recv()

    barrier = pltpu.get_barrier_semaphore()
    everyone = [partner, y_peer, hi_peer] + [cross_peer(i) for i in (1, 2, 3)]
    everyone += [x_peer(i) for i in (1, 2, 3)] + [z_peer(k) for k in (1, -1, 2, -2)]
    for device in everyone:
        pl.semaphore_signal(
            barrier, inc=1, device_id=device, device_id_type=pl.DeviceIdType.MESH
        )
    local = [
        pltpu.make_async_copy(row, row_v, loc.at[0]),
        pltpu.make_async_copy(col, col_v, loc.at[1]),
        pltpu.make_async_copy(tok, x_v.at[pl.ds(fi * 8, 8)], loc.at[2]),
        pltpu.make_async_copy(gate, gu_v.at[0], loc.at[3]),
        pltpu.make_async_copy(up, gu_v.at[1], loc.at[4]),
        pltpu.make_async_copy(down, w_v.at[0], loc.at[5]),
    ]
    for b in range(2):
        spot = xb.at[x * 2 + b, pl.ds(fi * 8, 8)]
        local.append(pltpu.make_async_copy(tok.at[:, block_of(b, 0)], spot, loc.at[6 + b]))
    for k in range(2):
        w_hbm = (gate, up)[k]
        local.append(
            pltpu.make_async_copy(
                w_hbm.at[early, block_of(y_hi, 0)], we.at[x, k], loc.at[8 + k]
            )
        )
        for b in range(2):
            local.append(
                pltpu.make_async_copy(
                    w_hbm.at[late, block_of(b, 0)], wl.at[x, k, b], loc.at[10 + 2 * k + b]
                )
            )
    for copy in local:
        copy.start()
    pl.semaphore_wait(barrier, len(everyone))

    def tokens_at(which, ff):
        if which == 0:
            return x_v.at[pl.ds(pl.multiple_of(ff * 8, 8), 8)]
        return xb.at[:, pl.ds(pl.multiple_of(ff * 8, 8), 8)]

    def z_copy(which, k, src=None):
        block = tokens_at(which, fi)
        return remote(
            block if src is None else src, block, snd.at[which], zr.at[which, k],
            z_peer(offset(k)),
        )

    def z_arrived(which, k):
        block = tokens_at(which, f_of(y_lo, (z - offset(k) + NZ) % NZ, core))
        remote(block, block, snd.at[which], zr.at[which, k], z_peer(offset(k))).wait_recv()

    def y_copy(which, k, yl):
        block = tokens_at(which, f_of(yl, (z - offset(k) + NZ) % NZ, core))
        return remote(block, block, snd.at[which], yr.at[k] if which == 0 else grp.at[8], y_peer)

    def c_copy(which, k, yl):
        block = tokens_at(which, f_of(yl, (z - offset(k) + NZ) % NZ, core))
        return remote(block, block, snd.at[which], grp.at[which], partner)

    def z_onward(which, k, to, slot):
        block = tokens_at(which, f_of(y_lo, (z - offset(k) + NZ) % NZ, core))
        return remote(block, block, snd.at[which], zr.at[which, slot], z_peer(offset(to)))


    local[2].wait()
    y_copy(0, 0, y_lo).start()
    for k in (1, 2, 3, 4):
        z_copy(0, k, tok).start()
    c_copy(0, 0, y_lo).start()

    small = []
    for i in (1, 3, 2):
        for b in range(2):
            small.append(
                remote(
                    tok.at[:, block_of(b, i)], xb.at[x * 2 + b, pl.ds(fi * 8, 8)],
                    snd.at[2], grp.at[2], x_peer(i),
                )
            )
    for i in range(NX):
        small.append(
            remote(
                tok.at[:, block_of(1 - y_hi, i)], xb.at[2 * NX + x, pl.ds(fi * 8, 8)],
                snd.at[2], grp.at[2], cross_peer(i),
            )
        )
    for copy in small:
        copy.start()
    down_copy = remote(down, w_v.at[1], snd.at[3], grp.at[3], partner)
    down_copy.start()

    def late_weight(i, k, b):
        return remote(
            (gate, up)[k].at[late, block_of(b, i)], wl.at[x, k, b],
            snd.at[8], grp.at[6], x_peer(i),
        )

    def early_weight(i, k):
        return remote(
            (gate, up)[k].at[early, block_of(y_hi, i)], we.at[x, k],
            snd.at[9], grp.at[7], x_peer(i),
        )

    def cross_weight(i, k):
        return remote(
            (gate, up)[k].at[early, block_of(1 - y_hi, i)], we.at[NX + x, k],
            snd.at[9], grp.at[7], cross_peer(i),
        )

    for i in (1, 3, 2):
        late_weight(i, 0, 0).start()
    for i in (1, 3):
        early_weight(i, 0).start()

    local[0].wait()
    local[1].wait()
    for k in range(2):
        codes = jnp.concatenate(
            [col_v[k : k + 1, :], jnp.zeros((1, 512 - FF), jnp.int32)], axis=1
        )
        colt[k] = jnp.broadcast_to(codes, (128, 512)).T

    def probe_rows(at, count):
        for k in range(2):
            @pl.loop(0, count)
            def _(t):
                rows = pl.ds(pl.multiple_of(at + t * 16, 16), 16)
                code = colt[k, rows, :]
                for d in range(0, D, 512):
                    wide = jnp.concatenate([code] * 4, axis=1)
                    bits = lax.population_count(
                        jnp.bitwise_and(wide, row_v[k : k + 1, d : d + 512])
                    )
                    sign = 1 - 2 * jnp.bitwise_and(bits, 1)
                    z_v[k, rows, d : d + 512] = sign.astype(F32).astype(BF16)

    def z_pass(which, k):
        z_arrived(which, k)
        if k == 3:
            z_onward(which, 3, 1, 5).start()

            @pl.when(core == 0)
            def _():
                z_onward(which, 3, 3, 7).start()

        if k == 4:
            z_onward(which, 4, 2, 6).start()

            @pl.when(core == 1)
            def _():
                z_onward(which, 4, 4, 7).start()

    def spread(which, k):
        y_copy(which, k, y_lo).start()
        c_copy(which, k, y_lo).start()

    probe_rows(0, 14)
    for k in (1, 2, 3, 4):
        z_pass(0, k)
        spread(0, k)
    probe_rows(224, 14)
    for k in (5, 6, 7):
        z_pass(0, k)
        spread(0, k)
    local[6].wait()
    local[7].wait()
    all_here(xb.at[0, pl.ds(0, 80)], 2)

    def on_y(k, carry):
        y_copy(0, k, 1 - y_lo).wait_recv()
        c_copy(0, k, 1 - y_lo).start()
        return carry

    lax.fori_loop(0, NZ, on_y, 0)
    for k in (3, 4, 1, 2):
        z_copy(1, k).start()
    local[3].wait()
    local[4].wait()
    all_here(x_v.at[pl.ds(0, 128)], 0)

    for k in range(2):
        cross_weight(1, k).start()
        late_weight(3, k, 1 - k).start()
        late_weight(1, k, 1 - k).start()
        cross_weight(3, k).start()
        cross_weight(2, k).start()
    for k in range(2):
        late_weight(2, k, 1 - k).start()
    for i in (1, 3, 2):
        late_weight(i, 1, 1).start()
    early_weight(2, 0).start()
    for i in (1, 3, 2):
        early_weight(i, 1).start()

    pre[...] = jnp.zeros_like(pre)

    @pl.loop(0, 4)
    def _(t):
        at = pl.ds(pl.multiple_of(t * 1024, 1024), 1024)
        toks = x_v[:, at]
        pre[0] += nt(gu_v[0, :, at], toks)
        pre[1] += nt(gu_v[1, :, at], toks)
        pre[2] += nt(z_v[0, :, at], toks)
        pre[3] += nt(z_v[1, :, at], toks)

    factor = D ** (-0.5)
    for at, n in ((0, 128), (128, 128), (256, 128), (384, 64)):
        a, b, da, db = (pre[k, at : at + n, :] * factor for k in range(4))
        s, s1, _ = activations(a)
        h = s * b
        dh = s1 * da * b + s * db
        hd[0, :, at : at + n] = h.T.astype(BF16)
        hd[1, :, at : at + n] = dh.T.astype(BF16)
    h_copy = remote(hd.at[1 - core], h_recv, snd.at[4], grp.at[4], partner)
    h_copy.start()
    for k in (3, 4):
        z_pass(1, k)
    local[5].wait()
    down_copy.wait_recv()
    h_copy.wait_recv()

    @pl.loop(0, 8)
    def _(t):
        at = pl.ds(pl.multiple_of(t * 512, 512), 512)
        total = nn(hd[core], w_v[0, :, at]) + nn(h_recv[...], w_v[1, :, at])
        yp[:, at] = total.astype(BF16)


    def piece(k, half):
        return pl.ds(pl.multiple_of(((z + k + NZ) % NZ) * 32 + 16 * half, 16), 16)

    half_rows = (slice(0, 16), slice(16, 32))

    def send_r(k, half):
        remote(
            yp.at[piece(k, half)], rs_r.at[4 - k, pl.ds(16 * half, 16)],
            snd.at[6], rrr.at[4 - k, half], right,
        ).start()

    def send_l(k, half):
        remote(
            yp.at[piece(-k, half)], rs_l.at[4 - k, pl.ds(16 * half, 16)],
            snd.at[6], rlr.at[4 - k, half], left,
        ).start()

    def add_r(k, half):
        slot = rs_r.at[3 - k, pl.ds(16 * half, 16)]
        remote(slot, slot, snd.at[6], rrr.at[3 - k, half], right).wait_recv()
        at = piece(k, half)
        yp[at, :] = (yp[at, :].astype(F32) + rs_r[3 - k, half_rows[half], :].astype(F32)).astype(BF16)

    def add_l(k, half):
        slot = rs_l.at[3 - k, pl.ds(16 * half, 16)]
        remote(slot, slot, snd.at[6], rlr.at[3 - k, half], left).wait_recv()
        at = piece(-k, half)
        yp[at, :] = (yp[at, :].astype(F32) + rs_l[3 - k, half_rows[half], :].astype(F32)).astype(BF16)

    send_r(4, 0)
    send_l(4, 1)
    send_r(3, 1)
    send_l(3, 0)
    add_r(3, 0)
    send_r(3, 0)
    add_l(3, 1)
    send_l(3, 1)
    for k in (2, 1):
        for half in (1, 0):
            add_r(k, half)
            send_r(k, half)
            add_l(k, 1 - half)
            send_l(k, 1 - half)
    mine = [piece(0, 0), piece(0, 1)]

    def y_exchange(half):
        return remote(
            yp.at[mine[half]], y_recv.at[pl.ds(16 * half, 16)], snd.at[6], er.at[half], y_peer
        )

    add_r(0, 1)
    add_l(0, 0)
    add_l(0, 1)
    y_exchange(1).start()
    add_r(0, 0)
    y_exchange(0).start()

    def gather_copy(k, half, sign):
        at = piece(-sign * (k - 1), half)
        sem = arr if sign == 1 else alr
        return remote(
            gy.at[at], gy.at[at], snd.at[7], sem.at[k - 1, half],
            right if sign == 1 else left,
        )

    def gather_arrived(k, half, sign):
        at = piece(-sign * k, half)
        sem = arr if sign == 1 else alr
        remote(
            gy.at[at], gy.at[at], snd.at[7], sem.at[k - 1, half],
            right if sign == 1 else left,
        ).wait_recv()

    for half in (1, 0):
        y_exchange(half).wait_recv()
        gy[mine[half], :] = (
            yp[mine[half], :].astype(F32) + y_recv[half_rows[half], :].astype(F32)
        ).astype(BF16)
        gather_copy(1, half, 1).start()
        gather_copy(1, half, -1).start()
    for k in (1, 2, 3, 4):
        for half in (1, 0):
            if k < 4 or half == 0:
                gather_arrived(k, half, 1)
            if k < 3 or (k == 3 and half == 0):
                gather_copy(k + 1, half, 1).start()
            if k < 4 or half == 1:
                gather_arrived(k, half, -1)
            if k < 3 or (k == 3 and half == 1):
                gather_copy(k + 1, half, -1).start()
        if k == 1:
            spread(1, 0)
            for j in (3, 4):
                spread(1, j)
            for j in (1, 2, 5, 6, 7):
                z_pass(1, j)
                spread(1, j)
            for j in range(2):
                cross_weight(0, j).start()
        if k == 2:
            num[...] = jnp.zeros_like(num)
            den[...] = jnp.zeros_like(den)
            sums[...] = jnp.zeros_like(sums)
            all_sent(x_v.at[pl.ds(0, 248)], 0)
            all_sent(xb.at[0, pl.ds(0, 80)], 2)
            all_sent(yp, 6)
            down_copy.wait_send()
            h_copy.wait_send()

    def from_gradient(side, out, rows):
        out[rows, :] = jnp.zeros((rows.size, TOK), F32)

        @pl.loop(0, 4)
        def _(t):
            at = pl.ds(pl.multiple_of(t * 1024, 1024), 1024)
            out[rows, :] += nt(w_v[side, rows, at], gy[:, at])

    def g_copy(group):
        rows = (late, early)[group]
        return remote(
            gp.at[rows], gg.at[core, rows], snd.at[5], (grp.at[5], grp.at[9])[group], partner
        )

    def gradients(at, n):
        rows = pl.ds(at, n)
        a, b, da, db = (pre[k, rows, :] * factor for k in range(4))
        gh, dgh = gg[0, rows, :], gg[1, rows, :]
        s, s1, s2 = activations(a)
        dga = dgh * b * s1 + gh * db * s1 + gh * b * s2 * da
        dgb = dgh * s + gh * s1 * da
        dg[x, 0, rows, :] = dga.astype(BF16)
        dg[x, 1, rows, :] = dgb.astype(BF16)

    def late_rows(r):
        return pl.ds(EARLY + r * ROWS, ROWS)

    def dg_copy(r, i, slot):
        rows = early if r == CHUNKS else late_rows(r)
        spot = dg.at[slot, :, rows]
        return remote(spot, spot, snd.at[10], dr.at[r, i], x_peer(i))

    def over_copy():
        return remote(dg.at[x, :, early], dgo.at[x], snd.at[10], dr.at[CHUNKS, 0], hi_peer)

    def onward_copy(i, slot):
        return remote(dgo.at[slot], dgo.at[slot], snd.at[10], dr.at[CHUNKS + 1, i], x_peer(i))

    def from_peer(i):
        return (x - i + NX) % NX

    def pass_on(cross, i):
        k, slot = (0, 1)[i == 3], from_peer(i)
        spot = dgo.at[slot, k] if cross else dg.at[slot, k, early]
        remote(spot, spot, snd.at[10], dr.at[CHUNKS + cross, 2], x_peer(i)).start()

    def means(group):
        rows = (late, early)[group]

        @pl.loop(0, 8)
        def _(t):
            at = pl.ds(pl.multiple_of(t * 512, 512), 512)
            for k in range(2):
                e = jnp.abs(nn(dg[x, k, rows, :], x_v[:, at]))
                sums[k, rows, :] += (e[:, :128] + e[:, 128:256]) + (e[:, 256:384] + e[:, 384:])

        for k in range(2):
            mean = jnp.sum(sums[k].T, axis=0, keepdims=True) * (1.0 / D)
            inverse = 1.0 / (mean + 1e-06)
            for t in range(4):
                at = 4 * k + t
                (scl, sc)[group][x, at : at + 1, :] = inverse[:, 128 * t : 128 * (t + 1)]

    def scl_copy(i, slot):
        return remote(scl.at[slot], scl.at[slot], snd.at[13], sr.at[2, i], x_peer(i))

    def sc_copy(i, slot):
        return remote(sc.at[slot], sc.at[slot], snd.at[11], sr.at[0, i], x_peer(i))

    def sc_over():
        return remote(sc.at[x], sc.at[NX + x], snd.at[11], sr.at[0, 0], hi_peer)

    def sc_onward(i, slot):
        return remote(sc.at[slot], sc.at[slot], snd.at[11], sr.at[1, i], x_peer(i))

    from_gradient(1, gp, late)
    g_copy(0).start()
    from_gradient(1, gp, early)
    g_copy(1).start()
    from_gradient(0, gg.at[core], late)

    def g_arrived(group):
        rows = (late, early)[group]
        remote(
            gp.at[rows], gg.at[1 - core, rows], snd.at[5], (grp.at[5], grp.at[9])[group], partner
        ).wait_recv()

    g_arrived(0)

    @pl.loop(0, LATE // 64)
    def _(t):
        gradients(pl.multiple_of(EARLY + t * 64, 64), 64)

    for i in (1, 3, 2):
        dg_copy(0, i, x).start()
    from_gradient(0, gg.at[core], early)
    g_arrived(1)

    @pl.loop(0, EARLY // 64)
    def _(t):
        gradients(pl.multiple_of(t * 64, 64), 64)

    over_copy().start()
    all_here(xb.at[:, pl.ds(0, 64)], 8)

    @pl.loop(0, NZ)
    def _(k):
        c_copy(1, k, 1 - y_lo).start()

    means(0)
    for i in (1, 3, 2):
        scl_copy(i, x).start()
    for r in range(1, CHUNKS):
        for i in (1, 3, 2):
            dg_copy(r, i, x).start()
    for i in (1, 3):
        dg_copy(CHUNKS, i, x).start()
    all_here(xb.at[:, pl.ds(0, 128)], 1)
    for copy in local[8:]:
        copy.wait()
    all_here(gu_v.at[0, pl.ds(0, 12 * LATE * BLK // D)], 6)

    def columns(ref, slot):
        pieces = [jnp.broadcast_to(ref[slot, t : t + 1, :], (128, 128)).T for t in range(8)]
        return [jnp.concatenate(pieces[4 * k : 4 * k + 4], axis=0) for k in range(2)]

    def add_terms(left_side, xs, scale, rows, b, weights):
        n = left_side.shape[1]
        hz = nn(left_side.reshape(2 * n, TOK), xs)
        for k in range(2):
            w = jnp.abs(hz[k * n : (k + 1) * n]) * jnp.concatenate([scale(k)] * 4, axis=1)
            den[b, k, rows, :] += w.astype(BF16).astype(F32)
            term = w * weights(k).astype(F32)
            num[b, k, rows, :] += term.astype(BF16).astype(F32)

    def part_copy(r):
        return remote(part.at[r], part_recv.at[r], snd.at[12], pr.at[r], hi_peer)

    for r in range(CHUNKS):
        rows = late_rows(r)

        @pl.loop(0, NX)
        def _(j):
            i = j ^ (j >> 1)
            peer = from_peer(i)

            @pl.when(i > 0)
            def _():
                if r == 0:
                    scl_copy(i, peer).wait_recv()
                dg_copy(r, i, peer).wait_recv()

            if r == 0:
                for k, column in enumerate(columns(scl, peer)):
                    sct[peer, k] = column
            for b in range(2):
                add_terms(
                    dg[peer, :, rows, :], xb[peer * 2 + b], lambda k: sct[peer, k, rows, :],
                    rows, b, lambda k: wl[peer, k, b, r * ROWS : (r + 1) * ROWS, :],
                )

        for k in range(2):
            part[r, k, 0] = num[1 - y_hi, k, rows, :].astype(BF16)
            part[r, k, 1] = den[1 - y_hi, k, rows, :].astype(BF16)
        part_copy(r).start()
        if r == 0:
            means(1)
            sc_over().start()
            for i in (1, 3, 2):
                sc_copy(i, x).start()
        if r == 2:
            over_copy().wait_recv()
            sc_over().wait_recv()
            for i in (1, 3):
                onward_copy(i, x).start()
            for i in (1, 3, 2):
                sc_onward(i, NX + x).start()

    all_here(gu_v.at[1, pl.ds(0, 14 * EARLY * BLK // D)], 7)

    def early_terms(cross, i):
        peer = from_peer(i)
        slot = NX * cross + peer
        if i:
            (sc_onward if cross else sc_copy)(i, slot).wait_recv()
        column = columns(sc, slot)
        add_terms(
            dgo[peer] if cross else dg[peer, :, early, :],
            xb[2 * NX + peer] if cross else xb[peer * 2 + y_hi],
            lambda k: column[k][:EARLY], early, y_hi, lambda k: we[slot, k],
        )

    early_terms(0, 0)
    for i in (1, 3):
        dg_copy(CHUNKS, i, from_peer(i)).wait_recv()
        pass_on(0, i)
    early_terms(1, 0)
    early_terms(0, 1)
    early_terms(0, 3)
    for i in (1, 3):
        onward_copy(i, from_peer(i)).wait_recv()
        pass_on(1, i)
    early_terms(1, 1)
    early_terms(1, 3)
    dg_copy(CHUNKS, 2, from_peer(2)).wait_recv()
    early_terms(0, 2)
    onward_copy(2, from_peer(2)).wait_recv()
    early_terms(1, 2)

    for k in range(2):
        n, d = num[y_hi, k, early, :], den[y_hi, k, early, :]
        out[k, early, :] = (n / jnp.maximum(d, 1.0)).astype(BF16)

    all_sent(xb.at[:, pl.ds(0, 248)], 1)
    all_sent(gu_v.at[0, pl.ds(0, 12 * LATE * BLK // D)], 8)
    all_sent(gu_v.at[1, pl.ds(0, 14 * EARLY * BLK // D)], 9)
    all_sent(gy.at[pl.ds(0, 224)], 7)
    all_sent(gu_v.at[0, pl.ds(0, (3 * LATE + 7 * EARLY) * 2 * TOK // D)], 10)
    all_sent(sc.at[pl.ds(0, 7)], 11)
    all_sent(scl.at[pl.ds(0, 3)], 13)
    all_sent(gp, 5)

    for r in range(CHUNKS):
        rows = late_rows(r)
        part_copy(r).wait_recv()
        for k in range(2):
            n = num[y_hi, k, rows, :] + part_recv[r, k, 0].astype(F32)
            d = den[y_hi, k, rows, :] + part_recv[r, k, 1].astype(F32)
            out[k, rows, :] = (n / jnp.maximum(d, 1.0)).astype(BF16)
    all_sent(part, 12)


def split_out(both, out_g, out_u, sems):
    copies = [
        pltpu.make_async_copy(both.at[k], (out_g, out_u)[k], sems.at[k]) for k in range(2)
    ]
    for copy in copies:
        copy.start()
    for copy in copies:
        copy.wait()


def on_device(tokens, gate_weight, up_weight, down_weight, row_code, col_code):
    vm = pltpu.VMEM
    scratch = [
        vm((2, FF, D), BF16),
        vm((2, FF, D), BF16),
        vm((2, FF, D), BF16),
        vm((TOK, D), BF16),
        vm((3 * NX, TOK, BLK), BF16),
        vm((2 * NX, 2, EARLY, BLK), BF16),
        vm((NX, 2, 2, LATE, BLK), BF16),
        vm((4, FF, TOK), F32),
        vm((2, TOK, FF), BF16),
        vm((TOK, FF), BF16),
        vm((TOK, D), BF16),
        vm((4, 32, D), BF16),
        vm((4, 32, D), BF16),
        vm((32, D), BF16),
        vm((TOK, D), BF16),
        vm((2, FF, TOK), F32),
        vm((FF, TOK), F32),
        vm((NX, 2, FF, TOK), BF16),
        vm((NX, 2, EARLY, TOK), BF16),
        vm((2, 512, 128), F32),
        vm((NX, 8, 128), F32),
        vm((2 * NX, 8, 128), F32),
        vm((NX, 2, 512, 128), F32),
        vm((2, 2, FF, BLK), F32),
        vm((2, 2, FF, BLK), F32),
        vm((CHUNKS, 2, 2, ROWS, BLK), BF16),
        vm((CHUNKS, 2, 2, ROWS, BLK), BF16),
        vm((2, D), jnp.int32),
        vm((2, FF), jnp.int32),
        vm((2, 512, 128), jnp.int32),
        DMA((14,)), DMA((14,)), DMA((10,)),
        DMA((2, NZ)), DMA((NZ,)),
        DMA((4, 2)), DMA((4, 2)), DMA((2,)),
        DMA((4, 2)), DMA((4, 2)),
        DMA((CHUNKS + 2, NX)), DMA((3, NX)), DMA((CHUNKS,)),
    ]
    hbm = pl.BlockSpec(memory_space=pltpu.HBM)
    both = pl.pallas_call(
        kernel,
        out_shape=pltpu.VMEM((2, FF, BLK), BF16),
        in_specs=[hbm] * 6,
        out_specs=pl.BlockSpec(memory_space=vm),
        scratch_shapes=scratch,
        compiler_params=pltpu.CompilerParams(
            collective_id=0, has_side_effects=True, vmem_limit_bytes=65_000_000
        ),
        name="merge",
    )(tokens[0], gate_weight[0], up_weight[0], down_weight[0], row_code[0], col_code[0])
    shape = jax.ShapeDtypeStruct((FF, BLK), BF16)
    return pl.pallas_call(
        split_out,
        out_shape=(shape, shape),
        in_specs=[pl.BlockSpec(memory_space=vm)],
        out_specs=(hbm, hbm),
        scratch_shapes=[DMA((2,))],
        compiler_params=pltpu.CompilerParams(vmem_limit_bytes=2_000_000),
        name="split_out",
    )(pltpu.with_memory_space_constraint(both, pltpu.VMEM))


def solution(mesh):
    return jax.shard_map(
        on_device,
        mesh=mesh,
        in_specs=(
            P("ckpt", "fsdp", None),
            P("ckpt", "fsdp", None),
            P("ckpt", "fsdp", None),
            P("ckpt", "fsdp", None),
            P("ckpt", None, None),
            P("ckpt", None, "fsdp"),
        ),
        out_specs=(P("fsdp", "ckpt"), P("fsdp", "ckpt")),
        check_vma=False,
    )
```

```python
import functools

import jax
import jax.numpy as jnp
from jax import lax
from jax.experimental import pallas as pl
from jax.experimental.pallas import tpu as pltpu
from jax.sharding import PartitionSpec as P

NX, NZ = 4, 8
D, FF, TOK = 4096, 448, 256
BLK = 512
EARLY = 208
LATE = FF - EARLY
ROWS = 48
CHUNKS = LATE // ROWS
F32, BF16 = jnp.float32, jnp.bfloat16
DMA = pltpu.SemaphoreType.DMA


def nt(left, right):
    return lax.dot_general(left, right, (((1,), (1,)), ((), ())), preferred_element_type=F32)


def nn(left, right):
    return jnp.dot(left, right, preferred_element_type=F32)


def remote(src, dst, send_sem, recv_sem, device):
    return pltpu.make_async_remote_copy(
        src_ref=src,
        dst_ref=dst,
        send_sem=send_sem,
        recv_sem=recv_sem,
        device_id=device,
        device_id_type=pl.DeviceIdType.MESH,
    )


def activations(a):
    q = lax.logistic(a)
    s = a * q
    s1 = q * (1.0 + a * (1.0 - q))
    s2 = q * (1.0 - q) * (2.0 + a * (1.0 - 2.0 * q))
    return s, s1, s2


def kernel(
    tok, gate, up, down, row, col, out,
    gu_v, w_v, z_v, x_v, xb, we, wl, pre, hd, h_recv, yp, rs_r, rs_l, y_recv, gy,
    gg, gp, dg, dgo, sums, scl, sc, sct, num, den, part, part_recv, row_v, col_v, colt,
    loc, snd, grp, zr, yr, rrr, rlr, er, arr, alr, dr, sr, pr,
):
    ci, fi = lax.axis_index("ckpt"), lax.axis_index("fsdp")
    y_hi, x = ci // NX, ci % NX
    y_lo, z, core = fi // (2 * NZ), (fi % (2 * NZ)) // 2, fi % 2
    row_base = y_lo * (2 * NZ)

    def f_of(yl, zz, cc):
        return (yl * NZ + zz) * 2 + cc

    me = (ci, fi)
    partner = (ci, f_of(y_lo, z, 1 - core))
    y_peer = (ci, f_of(1 - y_lo, z, core))
    hi_peer = ((1 - y_hi) * NX + x, fi)

    def x_peer(i):
        return (y_hi * NX + (x + i) % NX, fi)

    def cross_peer(i):
        return ((1 - y_hi) * NX + (x + i) % NX, fi)

    def block_of(b, i):
        return pl.ds(pl.multiple_of(BLK * (NX * b + (x + i) % NX), BLK), BLK)

    early, late = pl.ds(0, EARLY), pl.ds(EARLY, LATE)

    def z_peer(off):
        return (ci, f_of(y_lo, (z + off + NZ) % NZ, core))

    def offset(k):
        return ((k + 1) // 2) * (2 * (k % 2) - 1)

    right, left = z_peer(1), z_peer(-1)

    def all_sent(ref, sem):
        remote(ref, ref, snd.at[sem], grp.at[0], partner).wait_send()

    def all_here(ref, sem):
        remote(ref, ref, snd.at[0], grp.at[sem], partner).wait_recv()

    barrier = pltpu.get_barrier_semaphore()
    everyone = [partner, y_peer, hi_peer] + [cross_peer(i) for i in (1, 2, 3)]
    everyone += [x_peer(i) for i in (1, 2, 3)] + [z_peer(k) for k in (1, -1, 2, -2)]
    for device in everyone:
        pl.semaphore_signal(
            barrier, inc=1, device_id=device, device_id_type=pl.DeviceIdType.MESH
        )
    local = [
        pltpu.make_async_copy(row, row_v, loc.at[0]),
        pltpu.make_async_copy(col, col_v, loc.at[1]),
        pltpu.make_async_copy(tok, x_v.at[pl.ds(fi * 8, 8)], loc.at[2]),
        pltpu.make_async_copy(gate, gu_v.at[0], loc.at[3]),
        pltpu.make_async_copy(up, gu_v.at[1], loc.at[4]),
        pltpu.make_async_copy(down, w_v.at[0], loc.at[5]),
    ]
    for b in range(2):
        spot = xb.at[x * 2 + b, pl.ds(fi * 8, 8)]
        local.append(pltpu.make_async_copy(tok.at[:, block_of(b, 0)], spot, loc.at[6 + b]))
    for k in range(2):
        w_hbm = (gate, up)[k]
        local.append(
            pltpu.make_async_copy(
                w_hbm.at[early, block_of(y_hi, 0)], we.at[x, k], loc.at[8 + k]
            )
        )
        for b in range(2):
            local.append(
                pltpu.make_async_copy(
                    w_hbm.at[late, block_of(b, 0)], wl.at[x, k, b], loc.at[10 + 2 * k + b]
                )
            )
    for copy in local:
        copy.start()
    pl.semaphore_wait(barrier, len(everyone))

    def tokens_at(which, ff):
        if which == 0:
            return x_v.at[pl.ds(pl.multiple_of(ff * 8, 8), 8)]
        return xb.at[:, pl.ds(pl.multiple_of(ff * 8, 8), 8)]

    def z_copy(which, k, src=None):
        block = tokens_at(which, fi)
        return remote(
            block if src is None else src, block, snd.at[which], zr.at[which, k],
            z_peer(offset(k)),
        )

    def z_arrived(which, k):
        block = tokens_at(which, f_of(y_lo, (z - offset(k) + NZ) % NZ, core))
        remote(block, block, snd.at[which], zr.at[which, k], z_peer(offset(k))).wait_recv()

    def y_copy(which, k, yl):
        block = tokens_at(which, f_of(yl, (z - offset(k) + NZ) % NZ, core))
        return remote(block, block, snd.at[which], yr.at[k] if which == 0 else grp.at[8], y_peer)

    def c_copy(which, k, yl):
        block = tokens_at(which, f_of(yl, (z - offset(k) + NZ) % NZ, core))
        return remote(block, block, snd.at[which], grp.at[which], partner)

    def z_onward(which, k, to, slot):
        block = tokens_at(which, f_of(y_lo, (z - offset(k) + NZ) % NZ, core))
        return remote(block, block, snd.at[which], zr.at[which, slot], z_peer(offset(to)))


    local[2].wait()
    y_copy(0, 0, y_lo).start()
    for k in (1, 2, 3, 4):
        z_copy(0, k, tok).start()
    c_copy(0, 0, y_lo).start()

    small = []
    for i in (1, 3, 2):
        for b in range(2):
            small.append(
                remote(
                    tok.at[:, block_of(b, i)], xb.at[x * 2 + b, pl.ds(fi * 8, 8)],
                    snd.at[2], grp.at[2], x_peer(i),
                )
            )
    for i in range(NX):
        small.append(
            remote(
                tok.at[:, block_of(1 - y_hi, i)], xb.at[2 * NX + x, pl.ds(fi * 8, 8)],
                snd.at[2], grp.at[2], cross_peer(i),
            )
        )
    for copy in small:
        copy.start()
    down_copy = remote(down, w_v.at[1], snd.at[3], grp.at[3], partner)
    down_copy.start()

    def late_weight(i, k, b):
        return remote(
            (gate, up)[k].at[late, block_of(b, i)], wl.at[x, k, b],
            snd.at[8], grp.at[6], x_peer(i),
        )

    def early_weight(i, k):
        return remote(
            (gate, up)[k].at[early, block_of(y_hi, i)], we.at[x, k],
            snd.at[9], grp.at[7], x_peer(i),
        )

    def cross_weight(i, k):
        return remote(
            (gate, up)[k].at[early, block_of(1 - y_hi, i)], we.at[NX + x, k],
            snd.at[9], grp.at[7], cross_peer(i),
        )

    for i in (1, 3, 2):
        late_weight(i, 0, 0).start()
    for i in (1, 3):
        early_weight(i, 0).start()

    local[0].wait()
    local[1].wait()
    for k in range(2):
        codes = jnp.concatenate(
            [col_v[k : k + 1, :], jnp.zeros((1, 512 - FF), jnp.int32)], axis=1
        )
        colt[k] = jnp.broadcast_to(codes, (128, 512)).T

    def probe_rows(at, count):
        for k in range(2):
            @pl.loop(0, count)
            def _(t):
                rows = pl.ds(pl.multiple_of(at + t * 16, 16), 16)
                code = colt[k, rows, :]
                for d in range(0, D, 512):
                    wide = jnp.concatenate([code] * 4, axis=1)
                    bits = lax.population_count(
                        jnp.bitwise_and(wide, row_v[k : k + 1, d : d + 512])
                    )
                    sign = 1 - 2 * jnp.bitwise_and(bits, 1)
                    z_v[k, rows, d : d + 512] = sign.astype(F32).astype(BF16)

    def z_pass(which, k):
        z_arrived(which, k)
        if k == 3:
            z_onward(which, 3, 1, 5).start()

            @pl.when(core == 0)
            def _():
                z_onward(which, 3, 3, 7).start()

        if k == 4:
            z_onward(which, 4, 2, 6).start()

            @pl.when(core == 1)
            def _():
                z_onward(which, 4, 4, 7).start()

    def spread(which, k):
        y_copy(which, k, y_lo).start()
        c_copy(which, k, y_lo).start()

    probe_rows(0, 14)
    for k in (1, 2, 3, 4):
        z_pass(0, k)
        spread(0, k)
    probe_rows(224, 14)
    for k in (5, 6, 7):
        z_pass(0, k)
        spread(0, k)
    local[6].wait()
    local[7].wait()
    all_here(xb.at[0, pl.ds(0, 80)], 2)

    def on_y(k, carry):
        y_copy(0, k, 1 - y_lo).wait_recv()
        c_copy(0, k, 1 - y_lo).start()
        return carry

    lax.fori_loop(0, NZ, on_y, 0)
    for k in (3, 4, 1, 2):
        z_copy(1, k).start()
    local[3].wait()
    local[4].wait()
    all_here(x_v.at[pl.ds(0, 128)], 0)

    for k in range(2):
        cross_weight(1, k).start()
        late_weight(3, k, 1 - k).start()
        late_weight(1, k, 1 - k).start()
        cross_weight(3, k).start()
        cross_weight(2, k).start()
    for k in range(2):
        late_weight(2, k, 1 - k).start()
    for i in (1, 3, 2):
        late_weight(i, 1, 1).start()
    early_weight(2, 0).start()
    for i in (1, 3, 2):
        early_weight(i, 1).start()

    pre[...] = jnp.zeros_like(pre)

    @pl.loop(0, 4)
    def _(t):
        at = pl.ds(pl.multiple_of(t * 1024, 1024), 1024)
        toks = x_v[:, at]
        pre[0] += nt(gu_v[0, :, at], toks)
        pre[1] += nt(gu_v[1, :, at], toks)
        pre[2] += nt(z_v[0, :, at], toks)
        pre[3] += nt(z_v[1, :, at], toks)

    factor = D ** (-0.5)
    for at, n in ((0, 128), (128, 128), (256, 128), (384, 64)):
        a, b, da, db = (pre[k, at : at + n, :] * factor for k in range(4))
        s, s1, _ = activations(a)
        h = s * b
        dh = s1 * da * b + s * db
        hd[0, :, at : at + n] = h.T.astype(BF16)
        hd[1, :, at : at + n] = dh.T.astype(BF16)
    h_copy = remote(hd.at[1 - core], h_recv, snd.at[4], grp.at[4], partner)
    h_copy.start()
    for k in (3, 4):
        z_pass(1, k)
    local[5].wait()
    down_copy.wait_recv()
    h_copy.wait_recv()

    @pl.loop(0, 8)
    def _(t):
        at = pl.ds(pl.multiple_of(t * 512, 512), 512)
        total = nn(hd[core], w_v[0, :, at]) + nn(h_recv[...], w_v[1, :, at])
        yp[:, at] = total.astype(BF16)


    def piece(k, half):
        return pl.ds(pl.multiple_of(((z + k + NZ) % NZ) * 32 + 16 * half, 16), 16)

    half_rows = (slice(0, 16), slice(16, 32))

    def send_r(k, half):
        remote(
            yp.at[piece(k, half)], rs_r.at[4 - k, pl.ds(16 * half, 16)],
            snd.at[6], rrr.at[4 - k, half], right,
        ).start()

    def send_l(k, half):
        remote(
            yp.at[piece(-k, half)], rs_l.at[4 - k, pl.ds(16 * half, 16)],
            snd.at[6], rlr.at[4 - k, half], left,
        ).start()

    def add_r(k, half):
        slot = rs_r.at[3 - k, pl.ds(16 * half, 16)]
        remote(slot, slot, snd.at[6], rrr.at[3 - k, half], right).wait_recv()
        at = piece(k, half)
        yp[at, :] = (yp[at, :].astype(F32) + rs_r[3 - k, half_rows[half], :].astype(F32)).astype(BF16)

    def add_l(k, half):
        slot = rs_l.at[3 - k, pl.ds(16 * half, 16)]
        remote(slot, slot, snd.at[6], rlr.at[3 - k, half], left).wait_recv()
        at = piece(-k, half)
        yp[at, :] = (yp[at, :].astype(F32) + rs_l[3 - k, half_rows[half], :].astype(F32)).astype(BF16)

    send_r(4, 0)
    send_l(4, 1)
    send_r(3, 1)
    send_l(3, 0)
    add_r(3, 0)
    send_r(3, 0)
    add_l(3, 1)
    send_l(3, 1)
    for k in (2, 1):
        for half in (1, 0):
            add_r(k, half)
            send_r(k, half)
            add_l(k, 1 - half)
            send_l(k, 1 - half)
    mine = [piece(0, 0), piece(0, 1)]

    def y_exchange(half):
        return remote(
            yp.at[mine[half]], y_recv.at[pl.ds(16 * half, 16)], snd.at[6], er.at[half], y_peer
        )

    add_r(0, 1)
    add_l(0, 0)
    add_l(0, 1)
    y_exchange(1).start()
    add_r(0, 0)
    y_exchange(0).start()

    def gather_copy(k, half, sign):
        at = piece(-sign * (k - 1), half)
        sem = arr if sign == 1 else alr
        return remote(
            gy.at[at], gy.at[at], snd.at[7], sem.at[k - 1, half],
            right if sign == 1 else left,
        )

    def gather_arrived(k, half, sign):
        at = piece(-sign * k, half)
        sem = arr if sign == 1 else alr
        remote(
            gy.at[at], gy.at[at], snd.at[7], sem.at[k - 1, half],
            right if sign == 1 else left,
        ).wait_recv()

    for half in (1, 0):
        y_exchange(half).wait_recv()
        gy[mine[half], :] = (
            yp[mine[half], :].astype(F32) + y_recv[half_rows[half], :].astype(F32)
        ).astype(BF16)
        gather_copy(1, half, 1).start()
        gather_copy(1, half, -1).start()
    for k in (1, 2, 3, 4):
        for half in (1, 0):
            if k < 4 or half == 0:
                gather_arrived(k, half, 1)
            if k < 3 or (k == 3 and half == 0):
                gather_copy(k + 1, half, 1).start()
            if k < 4 or half == 1:
                gather_arrived(k, half, -1)
            if k < 3 or (k == 3 and half == 1):
                gather_copy(k + 1, half, -1).start()
        if k == 1:
            spread(1, 0)
            for j in (3, 4):
                spread(1, j)
            for j in (1, 2, 5, 6, 7):
                z_pass(1, j)
                spread(1, j)
            for j in range(2):
                cross_weight(0, j).start()
        if k == 2:
            num[...] = jnp.zeros_like(num)
            den[...] = jnp.zeros_like(den)
            sums[...] = jnp.zeros_like(sums)
            all_sent(x_v.at[pl.ds(0, 248)], 0)
            all_sent(xb.at[0, pl.ds(0, 80)], 2)
            all_sent(yp, 6)
            down_copy.wait_send()
            h_copy.wait_send()

    def from_gradient(side, out, rows):
        out[rows, :] = jnp.zeros((rows.size, TOK), F32)

        @pl.loop(0, 4)
        def _(t):
            at = pl.ds(pl.multiple_of(t * 1024, 1024), 1024)
            out[rows, :] += nt(w_v[side, rows, at], gy[:, at])

    def g_copy(group):
        rows = (late, early)[group]
        return remote(
            gp.at[rows], gg.at[core, rows], snd.at[5], (grp.at[5], grp.at[9])[group], partner
        )

    def gradients(at, n):
        rows = pl.ds(at, n)
        a, b, da, db = (pre[k, rows, :] * factor for k in range(4))
        gh, dgh = gg[0, rows, :], gg[1, rows, :]
        s, s1, s2 = activations(a)
        dga = dgh * b * s1 + gh * db * s1 + gh * b * s2 * da
        dgb = dgh * s + gh * s1 * da
        dg[x, 0, rows, :] = dga.astype(BF16)
        dg[x, 1, rows, :] = dgb.astype(BF16)

    def late_rows(r):
        return pl.ds(EARLY + r * ROWS, ROWS)

    def dg_copy(r, i, slot):
        rows = early if r == CHUNKS else late_rows(r)
        spot = dg.at[slot, :, rows]
        return remote(spot, spot, snd.at[10], dr.at[r, i], x_peer(i))

    def over_copy():
        return remote(dg.at[x, :, early], dgo.at[x], snd.at[10], dr.at[CHUNKS, 0], hi_peer)

    def onward_copy(i, slot):
        return remote(dgo.at[slot], dgo.at[slot], snd.at[10], dr.at[CHUNKS + 1, i], x_peer(i))

    def from_peer(i):
        return (x - i + NX) % NX

    def pass_on(cross, i):
        k, slot = (0, 1)[i == 3], from_peer(i)
        spot = dgo.at[slot, k] if cross else dg.at[slot, k, early]
        remote(spot, spot, snd.at[10], dr.at[CHUNKS + cross, 2], x_peer(i)).start()

    def means(group):
        rows = (late, early)[group]

        @pl.loop(0, 8)
        def _(t):
            at = pl.ds(pl.multiple_of(t * 512, 512), 512)
            n = rows.size
            both = jnp.abs(nn(dg[x, :, rows, :].reshape(2 * n, TOK), x_v[:, at]))
            for k in range(2):
                e = both[k * n : (k + 1) * n]
                sums[k, rows, :] += (e[:, :128] + e[:, 128:256]) + (e[:, 256:384] + e[:, 384:])

        for k in range(2):
            mean = jnp.sum(sums[k].T, axis=0, keepdims=True) * (1.0 / D)
            inverse = 1.0 / (mean + 1e-06)
            for t in range(4):
                at = 4 * k + t
                (scl, sc)[group][x, at : at + 1, :] = inverse[:, 128 * t : 128 * (t + 1)]

    def scl_copy(i, slot):
        return remote(scl.at[slot], scl.at[slot], snd.at[13], sr.at[2, i], x_peer(i))

    def sc_copy(i, slot):
        return remote(sc.at[slot], sc.at[slot], snd.at[11], sr.at[0, i], x_peer(i))

    def sc_over():
        return remote(sc.at[x], sc.at[NX + x], snd.at[11], sr.at[0, 0], hi_peer)

    def sc_onward(i, slot):
        return remote(sc.at[slot], sc.at[slot], snd.at[11], sr.at[1, i], x_peer(i))

    from_gradient(1, gp, late)
    g_copy(0).start()
    from_gradient(1, gp, early)
    g_copy(1).start()
    from_gradient(0, gg.at[core], late)

    def g_arrived(group):
        rows = (late, early)[group]
        remote(
            gp.at[rows], gg.at[1 - core, rows], snd.at[5], (grp.at[5], grp.at[9])[group], partner
        ).wait_recv()

    g_arrived(0)

    @pl.loop(0, LATE // 48)
    def _(t):
        gradients(pl.multiple_of(EARLY + t * 48, 16), 48)

    for i in (1, 3, 2):
        dg_copy(0, i, x).start()
    all_here(xb.at[:, pl.ds(0, 64)], 8)

    @pl.loop(0, NZ)
    def _(k):
        c_copy(1, k, 1 - y_lo).start()

    from_gradient(0, gg.at[core], early)
    g_arrived(1)

    @pl.loop(0, EARLY // 16)
    def _(t):
        gradients(pl.multiple_of(t * 16, 16), 16)

    over_copy().start()
    means(0)
    for i in (1, 3, 2):
        scl_copy(i, x).start()
    for r in range(1, CHUNKS):
        for i in (1, 3, 2):
            dg_copy(r, i, x).start()
    for i in (1, 3):
        dg_copy(CHUNKS, i, x).start()
    all_here(xb.at[:, pl.ds(0, 128)], 1)
    for copy in local[8:]:
        copy.wait()
    all_here(wl.at[pl.ds(0, 3)], 6)

    def columns(ref, slot):
        pieces = [jnp.broadcast_to(ref[slot, t : t + 1, :], (128, 128)).T for t in range(8)]
        return [jnp.concatenate(pieces[4 * k : 4 * k + 4], axis=0) for k in range(2)]

    def add_terms(left_side, xs, scale, rows, b, weights):
        n = left_side.shape[1]
        hz = nn(left_side.reshape(2 * n, TOK), xs)
        for k in range(2):
            w = jnp.abs(hz[k * n : (k + 1) * n]) * jnp.concatenate([scale(k)] * 4, axis=1)
            den[b, k, rows, :] += w.astype(BF16).astype(F32)
            term = w * weights(k).astype(F32)
            num[b, k, rows, :] += term.astype(BF16).astype(F32)

    def part_copy(r):
        return remote(part.at[r], part_recv.at[r], snd.at[12], pr.at[r], hi_peer)

    for r in range(CHUNKS):
        rows = late_rows(r)

        @pl.loop(0, NX)
        def _(j):
            i = j ^ (j >> 1)
            peer = from_peer(i)

            @pl.when(i > 0)
            def _():
                if r == 0:
                    scl_copy(i, peer).wait_recv()
                dg_copy(r, i, peer).wait_recv()

            if r == 0:
                for k, column in enumerate(columns(scl, peer)):
                    sct[peer, k] = column
            for b in range(2):
                add_terms(
                    dg[peer, :, rows, :], xb[peer * 2 + b], lambda k: sct[peer, k, rows, :],
                    rows, b, lambda k: wl[peer, k, b, r * ROWS : (r + 1) * ROWS, :],
                )

        for k in range(2):
            part[r, k, 0] = num[1 - y_hi, k, rows, :].astype(BF16)
            part[r, k, 1] = den[1 - y_hi, k, rows, :].astype(BF16)
        part_copy(r).start()
        if r == 0:
            means(1)
            sc_over().start()
            for i in (1, 3, 2):
                sc_copy(i, x).start()
        if r == 2:
            over_copy().wait_recv()
            sc_over().wait_recv()
            for i in (1, 3):
                onward_copy(i, x).start()
            for i in (1, 3, 2):
                sc_onward(i, NX + x).start()

    all_here(we.at[pl.ds(0, 7)], 7)

    def early_terms(cross, i):
        peer = from_peer(i)
        slot = NX * cross + peer
        if i:
            (sc_onward if cross else sc_copy)(i, slot).wait_recv()
        column = columns(sc, slot)
        add_terms(
            dgo[peer] if cross else dg[peer, :, early, :],
            xb[2 * NX + peer] if cross else xb[peer * 2 + y_hi],
            lambda k: column[k][:EARLY], early, y_hi, lambda k: we[slot, k],
        )

    early_terms(0, 0)
    for i in (1, 3):
        dg_copy(CHUNKS, i, from_peer(i)).wait_recv()
        pass_on(0, i)
    early_terms(1, 0)
    early_terms(0, 1)
    early_terms(0, 3)
    for i in (1, 3):
        onward_copy(i, from_peer(i)).wait_recv()
        pass_on(1, i)
    early_terms(1, 1)
    early_terms(1, 3)
    dg_copy(CHUNKS, 2, from_peer(2)).wait_recv()
    early_terms(0, 2)
    onward_copy(2, from_peer(2)).wait_recv()
    early_terms(1, 2)

    for k in range(2):
        n, d = num[y_hi, k, early, :], den[y_hi, k, early, :]
        out[k, early, :] = (n / jnp.maximum(d, 1.0)).astype(BF16)

    all_sent(xb.at[:, pl.ds(0, 248)], 1)
    all_sent(wl.at[pl.ds(0, 3)], 8)
    all_sent(we.at[pl.ds(0, 7)], 9)
    all_sent(gy.at[pl.ds(0, 224)], 7)
    all_sent(gu_v.at[0, pl.ds(0, (3 * LATE + 7 * EARLY) * 2 * TOK // D)], 10)
    all_sent(sc.at[pl.ds(0, 7)], 11)
    all_sent(scl.at[pl.ds(0, 3)], 13)
    all_sent(gp, 5)

    for r in range(CHUNKS):
        rows = late_rows(r)
        part_copy(r).wait_recv()
        for k in range(2):
            n = num[y_hi, k, rows, :] + part_recv[r, k, 0].astype(F32)
            d = den[y_hi, k, rows, :] + part_recv[r, k, 1].astype(F32)
            out[k, rows, :] = (n / jnp.maximum(d, 1.0)).astype(BF16)
    all_sent(part, 12)


def split_out(both, out_g, out_u, sems):
    copies = [
        pltpu.make_async_copy(both.at[k], (out_g, out_u)[k], sems.at[k]) for k in range(2)
    ]
    for copy in copies:
        copy.start()
    for copy in copies:
        copy.wait()


def on_device(tokens, gate_weight, up_weight, down_weight, row_code, col_code):
    vm = pltpu.VMEM
    scratch = [
        vm((2, FF, D), BF16),
        vm((2, FF, D), BF16),
        vm((2, FF, D), BF16),
        vm((TOK, D), BF16),
        vm((3 * NX, TOK, BLK), BF16),
        vm((2 * NX, 2, EARLY, BLK), BF16),
        vm((NX, 2, 2, LATE, BLK), BF16),
        vm((4, FF, TOK), F32),
        vm((2, TOK, FF), BF16),
        vm((TOK, FF), BF16),
        vm((TOK, D), BF16),
        vm((4, 32, D), BF16),
        vm((4, 32, D), BF16),
        vm((32, D), BF16),
        vm((TOK, D), BF16),
        vm((2, FF, TOK), F32),
        vm((FF, TOK), F32),
        vm((NX, 2, FF, TOK), BF16),
        vm((NX, 2, EARLY, TOK), BF16),
        vm((2, 512, 128), F32),
        vm((NX, 8, 128), F32),
        vm((2 * NX, 8, 128), F32),
        vm((NX, 2, 512, 128), F32),
        vm((2, 2, FF, BLK), F32),
        vm((2, 2, FF, BLK), F32),
        vm((CHUNKS, 2, 2, ROWS, BLK), BF16),
        vm((CHUNKS, 2, 2, ROWS, BLK), BF16),
        vm((2, D), jnp.int32),
        vm((2, FF), jnp.int32),
        vm((2, 512, 128), jnp.int32),
        DMA((14,)), DMA((14,)), DMA((10,)),
        DMA((2, NZ)), DMA((NZ,)),
        DMA((4, 2)), DMA((4, 2)), DMA((2,)),
        DMA((4, 2)), DMA((4, 2)),
        DMA((CHUNKS + 2, NX)), DMA((3, NX)), DMA((CHUNKS,)),
    ]
    hbm = pl.BlockSpec(memory_space=pltpu.HBM)
    both = pl.pallas_call(
        kernel,
        out_shape=pltpu.VMEM((2, FF, BLK), BF16),
        in_specs=[hbm] * 6,
        out_specs=pl.BlockSpec(memory_space=vm),
        scratch_shapes=scratch,
        compiler_params=pltpu.CompilerParams(
            collective_id=0, has_side_effects=True, vmem_limit_bytes=65_000_000
        ),
        name="merge",
    )(tokens[0], gate_weight[0], up_weight[0], down_weight[0], row_code[0], col_code[0])
    shape = jax.ShapeDtypeStruct((FF, BLK), BF16)
    return pl.pallas_call(
        split_out,
        out_shape=(shape, shape),
        in_specs=[pl.BlockSpec(memory_space=vm)],
        out_specs=(hbm, hbm),
        scratch_shapes=[DMA((2,))],
        compiler_params=pltpu.CompilerParams(vmem_limit_bytes=2_000_000),
        name="split_out",
    )(pltpu.with_memory_space_constraint(both, pltpu.VMEM))


def solution(mesh):
    return jax.shard_map(
        on_device,
        mesh=mesh,
        in_specs=(
            P("ckpt", "fsdp", None),
            P("ckpt", "fsdp", None),
            P("ckpt", "fsdp", None),
            P("ckpt", "fsdp", None),
            P("ckpt", None, None),
            P("ckpt", None, "fsdp"),
        ),
        out_specs=(P("fsdp", "ckpt"), P("fsdp", "ckpt")),
        check_vma=False,
    )
```
